128 devices in a mesh: grp: 8 (over x_hi, z), mem: 16 (over y, x_lo, core).
Axes of the slice: x: 4 (x_hi: 2, x_lo: 2; x = x_hi * 2 + x_lo), y: 4, z: 4, core: 2. Of those that a mesh axis runs over, the one named last changes fastest.
Arguments:
- candidates: bfloat16 [131072, 4096], P(('grp', 'mem')), may hold values from -1 to 1
- round_one: bfloat16 [8192, 4096], P(('grp', 'mem')), may hold values from -1 to 1
- counts: int32 [8, 16], P('grp', 'mem'), may hold values from 1 to 64, 384 in all within a row
- chosen: int32 [8, 128], P('grp'), may hold values from 0 to 383, as said below
Outputs:
- group_dist: float32 [131072], P(('grp', 'mem'))
- final_dist: float32 [131072], P(('grp', 'mem'))
The draws below stay inside these ranges and needn't reach their ends.
Inputs may be any that keep to these rules, and one draw needn't show every extreme that they name: In each group the counts sum to 384, and some device of each group has exactly 64. `chosen`: within a group the 128 positions are distinct, each below 384.
All inputs are finite; a program needn't handle non-finite values.
Results may differ from the reference program's by a relative error of at most 0.0003.
Values may be sent and summed in bfloat16 or wider, within the bound.
A program may use at most 128 MiB of HBM per device.

```python
import math
import jax
import jax.numpy as jnp
import numpy as np
from jax import lax

EMBED_DIM = 4096
ROWS_DEV = 1024
ROUND_MAX = 64
KCENTERS = 128
GROUP_CENTERS = 384
ROWS_ALL = 131072
SLOTS_ALL = 8192
N_GRP = 8
N_MEM = 16


def center_table(key):
    table_key = jax.random.fold_in(key, 101)
    entry_key, scale_key = jax.random.split(table_key)
    entries = jnp.clip(jax.random.normal(entry_key, (SLOTS_ALL, EMBED_DIM), jnp.float32), -4.0, 4.0)
    row_scale = jnp.exp(jax.random.uniform(scale_key, (SLOTS_ALL,), jnp.float32, math.log(0.7), math.log(1.4)))
    return entries * (row_scale[:, None] / math.sqrt(EMBED_DIM))


def draw_round_one(key, part):
    return center_table(key).astype(jnp.bfloat16)


def draw_candidates(key, part):
    table = center_table(key)
    pick_key = jax.random.fold_in(key, 203)
    own_key, any_key, side_key, noise_key, level_key = jax.random.split(pick_key, 5)
    group_slots = ROUND_MAX * N_MEM
    row_ids = jnp.arange(ROWS_ALL, dtype=jnp.int32)
    home = row_ids // (ROWS_DEV * N_MEM)
    own_source = home * group_slots + jax.random.randint(own_key, (ROWS_ALL,), 0, group_slots)
    any_source = jax.random.randint(any_key, (ROWS_ALL,), 0, SLOTS_ALL)
    side = jax.random.randint(side_key, (ROWS_ALL,), 0, 2)
    source = jnp.where(side == 0, own_source, any_source).astype(jnp.int32)
    level = jnp.exp(jax.random.uniform(level_key, (ROWS_ALL,), jnp.float32, math.log(0.15), math.log(0.5)))
    noise = jnp.clip(jax.random.normal(noise_key, (ROWS_ALL, EMBED_DIM), jnp.float32), -4.0, 4.0)
    rows = table[source] + noise * (level[:, None] / math.sqrt(EMBED_DIM))
    return rows.astype(jnp.bfloat16)


def draw_chosen(key, part):
    group_keys = jax.random.split(key, N_GRP + 2)

    def one_group(group_key):
        return jax.random.permutation(group_key, GROUP_CENTERS - 1)[:KCENTERS]
    drawn_ids = jax.vmap(one_group)(group_keys[:N_GRP]).astype(jnp.int32)
    target_group = jax.random.randint(group_keys[N_GRP], (), 0, N_GRP)
    target_slot = jax.random.randint(group_keys[N_GRP + 1], (), 0, KCENTERS)
    group_ids = jnp.arange(N_GRP, dtype=jnp.int32)[:, None]
    slot_ids = jnp.arange(KCENTERS, dtype=jnp.int32)[None, :]
    replace_here = (group_ids == target_group) & (slot_ids == target_slot)
    return jnp.where(replace_here, GROUP_CENTERS - 1, drawn_ids).astype(jnp.int32)


def length_profile(amount, total, bound, slope):
    weights = [(1 << 20) // math.isqrt(standing ** slope) + 1 for standing in range(2, amount + 1)]
    rest, given = total - bound - (amount - 1), [1] * (amount - 1)
    while rest > 0:
        free = [i for i in range(amount - 1) if given[i] < bound]
        mass, budget = sum([weights[i] for i in free]), rest
        for i in free:
            extra = min(bound - given[i], max(1, budget * weights[i] // mass), rest)
            given[i] = given[i] + extra
            rest = rest - extra
    return np.array([bound] + given)


def ragged_sizes(rng, number_of, total, limit, lean):
    if number_of == 2:
        one = jax.random.randint(rng, (), max(1, total - limit), min(limit, total - 1) + 1)
        return jnp.stack([one, total - one])
    tallies = jnp.asarray(length_profile(number_of, total, limit, lean), jnp.int32)
    twos = (number_of - 1) // 2
    giver, sink = tallies[1:1 + 2 * twos:2], tallies[2:2 + 2 * twos:2]
    room = jnp.minimum(giver - 1, limit - sink)
    shifted = jax.random.randint(jax.random.fold_in(rng, 1), (twos,), 0, 1 << 20) % (room + 1)
    tallies = tallies.at[1:1 + 2 * twos:2].set(giver - shifted).at[2:2 + 2 * twos:2].set(sink + shifted)
    return tallies[jax.random.permutation(jax.random.fold_in(rng, 2), number_of)]


def setup_inputs(seed: int = 0) -> dict:
    arg_keys = jax.random.split(jax.random.key(seed), 5)
    return {
        "candidates": draw_candidates(jax.random.fold_in(arg_keys[4], 71), 0),
        "round_one": draw_round_one(jax.random.fold_in(arg_keys[4], 71), 0),
        "counts": jax.vmap(lambda own: ragged_sizes(own, N_MEM, GROUP_CENTERS, ROUND_MAX, 2))(jax.random.split(arg_keys[2], N_GRP)).reshape((N_GRP, N_MEM)).astype(jnp.int32),
        "chosen": draw_chosen(jax.random.fold_in(arg_keys[4], 71), 0),
    }


def sq_norms(matrix):
    return jnp.sum(jnp.square(matrix.astype(jnp.float32)), axis=1)


def distances(cand_rows, cand_norm, center_rows):
    inner = lax.dot_general(cand_rows, center_rows, (((1,), (1,)), ((), ())), preferred_element_type=jnp.float32)
    return (cand_norm[:, None] + sq_norms(center_rows)[None, :]) - 2.0 * inner


def reference(candidates, round_one, counts, chosen):
    slot_total = N_MEM * ROUND_MAX
    cand_groups = candidates.reshape(N_GRP, N_MEM * ROWS_DEV, EMBED_DIM)
    center_groups = round_one.reshape(N_GRP, slot_total, EMBED_DIM)
    slot_ids = jnp.arange(slot_total, dtype=jnp.int32)
    within = slot_ids % ROUND_MAX
    holder = slot_ids // ROUND_MAX

    def group_work(inputs):
        cand_rows, center_rows, group_counts, picked_ids = inputs
        offsets = jnp.cumsum(group_counts) - group_counts
        usable = within < group_counts[holder]
        position = offsets[holder] + within
        gaps = distances(cand_rows, sq_norms(cand_rows), center_rows)
        gaps = jnp.where(usable[None, :], gaps, jnp.inf)
        nearest = jnp.min(gaps, axis=1)
        select = ((picked_ids[:, None] == position[None, :]) & usable[None, :]).astype(jnp.float32)
        picked = jnp.dot(select, center_rows.astype(jnp.float32), precision=lax.Precision.HIGHEST).astype(jnp.bfloat16)
        return nearest, picked

    nearest, picked = lax.map(group_work, (cand_groups, center_groups, counts, chosen))
    every_center = picked.reshape(N_GRP * KCENTERS, EMBED_DIM)

    def final_work(cand_rows):
        return jnp.min(distances(cand_rows, sq_norms(cand_rows), every_center), axis=1)

    final = lax.map(final_work, cand_groups)
    return nearest.reshape(-1), final.reshape(-1)
```

```python
import functools

import jax
import jax.numpy as jnp
from jax import lax
from jax.experimental import pallas as pl
from jax.experimental.pallas import tpu as pltpu
from jax.sharding import PartitionSpec as P

MESH = pl.DeviceIdType.MESH
NT = (((1,), (1,)), ((), ()))
F32 = jnp.float32
BF16 = jnp.bfloat16

ROWS = 1024
WIDTH = 4096
HALF = WIDTH // 2
SLOTS = 64
PICKS = 128
CHIPS = 8
SHARE = PICKS // CHIPS
REST = 32

SHARES = (
    (1, 0, 2, 0, 1024),
    (0, 2, 1, 1024, 1536),
    (1, 2, 0, 1536, 2048),
)


def place():
    g, m = lax.axis_index("grp"), lax.axis_index("mem")
    x = (g // 4) * 2 + (m // 2) % 2
    return x, m // 4, g % 4, m % 2


def device(x, y, z, c):
    return {"grp": (x // 2) * 4 + z, "mem": y * 4 + (x % 2) * 2 + c}


def kernel(
    cand_ref, slot_ref, count_ref, chosen_ref, near_ref, final_ref,
    A, S, CN, M1, M2, R1, R2, FIN, UN, D, NRM, DU, AN,
    local_sem, send_sem, recv_sem,
):
    x, y, z, c = place()
    pos3 = (x, y, z)
    xl = x % 2
    other = 1 - c
    me = lax.axis_index("mem")
    chip = y * 2 + xl
    counter = [0]

    def shifted(dim, o):
        p = list(pos3)
        p[dim] = (p[dim] + o) % 4
        return device(p[0], p[1], p[2], c)

    def in_group(dy, dx, dc):
        return device(x - xl + (xl + dx) % 2, (y + dy) % 4, z, (c + dc) % 2)

    def send(src, dst, dev):
        n = counter[0]
        counter[0] += 1
        cp = pltpu.make_async_remote_copy(
            src_ref=src, dst_ref=dst, send_sem=send_sem.at[n], recv_sem=recv_sem.at[n],
            device_id=dev, device_id_type=MESH,
        )
        cp.start()
        sent.append(cp)
        return cp

    sent = []
    sibling = device(x, y, z, other)

    loads = []
    mine = pltpu.make_async_copy(
        slot_ref.at[:, pl.ds(pl.multiple_of(c * HALF, HALF), HALF)], S.at[c], local_sem.at[0])
    mine.start()
    for h in range(2):
        cp = pltpu.make_async_copy(cand_ref.at[:, h * HALF:(h + 1) * HALF], A.at[h], local_sem.at[1 + h])
        cp.start()
        loads.append(cp)

    group_peers = [(dy, dx, dc) for dy in range(4) for dx in range(2) for dc in range(2) if dy or dx or dc]
    partners = [in_group(*o) for o in group_peers]
    partners += [shifted(2, o) for o in (1, 2, 3)]
    partners += [device((x // 2 * 2 + 2 + i) % 4, y, z, c) for i in (0, 1)]
    barrier = pltpu.get_barrier_semaphore()
    for dev in partners:
        pl.semaphore_signal(barrier, inc=1, device_id=dev, device_id_type=MESH)
    CN[me] = jnp.broadcast_to(count_ref[...], (8, 128))
    pl.semaphore_wait(barrier, len(partners))

    count_copies = [send(CN.at[me], CN.at[me], in_group(*o)) for o in group_peers]
    slot_copy = send(
        slot_ref.at[:, pl.ds(pl.multiple_of(other * HALF, HALF), HALF)], S.at[c], sibling)

    D[...] = jnp.zeros_like(D)
    NRM[...] = jnp.zeros_like(NRM)

    def fold(b):
        b = b.astype(F32)
        b = b * b
        total = b[:, 0:128]
        for k in range(128, b.shape[1], 128):
            total = total + b[:, k:k + 128]
        return total

    for cp in count_copies:
        cp.wait_recv()
    lane = lax.broadcasted_iota(jnp.int32, (1, 128), 1)
    row16 = lax.broadcasted_iota(jnp.int32, (16, 128), 0)
    row128 = lax.broadcasted_iota(jnp.int32, (128, 128), 0)
    cnt = jnp.max(CN[...].astype(F32), axis=1)
    off = jnp.zeros((16, 128), F32)
    for m in range(15):
        off = off + jnp.where(row16 > m, cnt[m:m + 1, :], 0.0)

    def pick(table, index):
        return jnp.sum(jnp.where(row16 == index, table, 0.0), axis=0, keepdims=True)

    chosen_col = jnp.transpose(jnp.broadcast_to(chosen_ref[...].astype(F32), (128, 128)))

    def below(p):
        return jnp.sum(jnp.where(chosen_col < p, 1.0, 0.0), axis=0, keepdims=True)

    def whole(v):
        return v.astype(jnp.int32)

    first_off = pick(off, 2 * chip)
    second = lane >= SLOTS
    within = lane % SLOTS
    start = jnp.where(second, pick(off, 2 * chip + 1), first_off)
    live = jnp.where(second, pick(cnt, 2 * chip + 1), pick(cnt, 2 * chip))
    spot = start + within.astype(F32)
    alive = within.astype(F32) < live
    is_chosen = jnp.sum(jnp.where(chosen_col == spot, 1.0, 0.0), axis=0, keepdims=True) > 0.5
    q, q0 = whole(below(spot)), whole(below(first_off))
    u, u0 = whole(spot) - q, whole(first_off) - q0
    key1 = jnp.where(alive, jnp.where(is_chosen, (q % 8) * 16 + (q - q0) // 8, -1), -1)
    key2 = jnp.where(alive, jnp.where(is_chosen, -1, (u % 8) * 16 + (u - u0) // 8), -1)
    hot1 = jnp.where(row128 == key1, 1.0, 0.0).astype(BF16)
    hot2 = jnp.where(row128 == key2, 1.0, 0.0).astype(BF16)

    mine.wait()
    slot_copy.wait_recv()
    held = S[...].reshape(2 * SLOTS, HALF)
    M1[...] = jnp.dot(hot1, held, preferred_element_type=F32).astype(BF16).reshape(CHIPS, 16, HALF)
    chip_peers = [(dy, dx) for dy in range(4) for dx in range(2) if dy or dx]

    def target(dy, dx):
        return (y + dy) % 4 * 2 + (xl + dx) % 2

    swap1 = [send(M1.at[target(*o)], R1.at[chip], in_group(*o, 0)) for o in chip_peers]
    M2[...] = jnp.dot(hot2, held, preferred_element_type=F32).astype(BF16).reshape(CHIPS, 16, HALF)
    R1[chip] = M1[chip]
    R2[chip] = M2[chip]

    source = lane // 16
    low = jnp.sum(jnp.where(row16 == 2 * source, off, 0.0), axis=0, keepdims=True)
    high = jnp.sum(jnp.where(row16 == 2 * source + 1, off + cnt, 0.0), axis=0, keepdims=True)
    ql, qh = whole(below(low)), whole(below(high))
    ul, uh = whole(low) - ql, whole(high) - qh

    def take(lo, hi, rows):
        at = lo + (chip - lo + 1024) % 8 + 8 * (lane % 16)
        key = jnp.where(at < hi, at // 8, -1)
        rowid = lax.broadcasted_iota(jnp.int32, (rows, 128), 0)
        return jnp.where(rowid == key, 1.0, 0.0).astype(BF16)

    take1, take2 = take(ql, qh, SHARE), take(ul, uh, REST)

    for cp in loads:
        cp.wait()
    for i in range(8):
        rows = slice(i * 128, (i + 1) * 128)
        part = fold(A[0, rows, :]) + fold(A[1, rows, :])
        AN[0:1, rows] = jnp.sum(jnp.transpose(part), axis=0, keepdims=True)

    for cp in swap1:
        cp.wait_recv()
    own = jnp.dot(take1, R1[...].reshape(CHIPS * 16, HALF), preferred_element_type=F32)
    FIN[c, x, y, z] = own.astype(BF16)

    def block(share, s1, s2, s3):
        d1, d2, d3, lo, hi = share
        sel = [None] * 3
        sel[d1], sel[d2], sel[d3] = s1, s2, s3
        return (c, *sel, slice(None), slice(lo, hi))

    ALL = slice(None)

    def cast(share, index, dim, o):
        ref = FIN.at[block(share, *index)]
        return send(ref, ref, shifted(dim, o))

    def relay(share, index):
        ref = FIN.at[block(share, *index)]
        return send(ref, ref, sibling)

    def at(share, k, o):
        return (pos3[share[k]] + o) % 4

    n = len(SHARES)
    local = [[] for _ in range(n)]
    first = []
    for s in SHARES:
        here = (at(s, 0, 0), at(s, 1, 0), at(s, 2, 0))
        first.append([cast(s, here, s[0], o) for o in (1, 3, 2)])
    own_ref = FIN.at[c, x, y, z]
    own_relay = send(own_ref, own_ref, sibling)
    swap2 = [send(M2.at[target(*o)], R2.at[chip], in_group(*o, 0)) for o in chip_peers]

    line = [[[] for _ in range(4)] for _ in range(n)]
    seconds = []
    for i, s in enumerate(SHARES):
        for o, cp in zip((1, 3, 2), first[i]):
            cp.wait_recv()
            local[i].append(relay(s, (at(s, 0, -o), at(s, 1, 0), at(s, 2, 0))))
        row = (ALL, at(s, 1, 0), at(s, 2, 0))
        seconds.append([cast(s, row, s[1], o) for o in (1, 3, 2)])
        line[i][0] = [cast(s, row, s[2], 1), cast(s, row, s[2], 3)]

    for cp in swap2:
        cp.wait_recv()
    UN[c, y, xl] = jnp.dot(
        take2, R2[...].reshape(CHIPS * 16, HALF), preferred_element_type=F32).astype(BF16)
    cut = HALF // 2
    left, right = slice(0, cut), slice(cut, HALF)
    un_relay = []

    def un_send(sel, dev):
        ref = UN.at[sel]
        return send(ref, ref, dev)

    un_relay.append(un_send((c, y, xl), sibling))
    un_y = [un_send((c, y, xl, ALL, left), in_group(o, 0, 0)) for o in (1, 3, 2)]
    un_x = un_send((c, y, xl, ALL, right), in_group(0, 1, 0))

    for j, o in enumerate((1, 3, 2)):
        for i, s in enumerate(SHARES):
            seconds[i][j].wait_recv()
            row = (ALL, at(s, 1, -o), at(s, 2, 0))
            line[i][1 + j] = [cast(s, row, s[2], 1), cast(s, row, s[2], 3)]
            local[i].append(relay(s, row))

    un_x.wait_recv()
    un_relay.append(un_send((c, y, 1 - xl, ALL, right), sibling))
    un_xy = [un_send((c, y, ALL, ALL, right), in_group(o, 0, 0)) for o in (1, 3, 2)]
    for o, cp in zip((1, 3, 2), un_y):
        cp.wait_recv()
        un_relay.append(un_send((c, (y + 4 - o) % 4, xl, ALL, left), sibling))
    un_yx = un_send((c, ALL, xl, ALL, left), in_group(0, 1, 0))

    def plane(share, p, rows=None):
        d3, lo, hi = share[2], share[3], share[4]
        sel = [ALL, ALL, ALL]
        sel[d3] = p
        where = tuple(sel) + (ALL,)
        total = D[where + (ALL,)].reshape(256, ROWS)
        norm = NRM[where + (ALL,)].reshape(256, 128)
        for h in range(2):
            b = FIN[(h,) + where + (slice(lo, hi),)].reshape(256, hi - lo)
            total = total + lax.dot_general(b, A[h, :, lo:hi], NT, preferred_element_type=F32)
            norm = norm + fold(b)
        D[where + (ALL,)] = total.reshape(4, 4, 16, ROWS)
        NRM[where + (ALL,)] = norm.reshape(4, 4, 16, 128)

    own_relay.wait_recv()
    for i, s in enumerate(SHARES):
        for cp in local[i]:
            cp.wait_recv()
        plane(s, at(s, 2, 0))

    relays = [[[], []] for _ in range(n)]
    onward = [[[], []] for _ in range(n)]
    for j, o2 in enumerate((0, 1, 3, 2)):
        for i, s in enumerate(SHARES):
            for k, o in enumerate((1, 3)):
                line[i][j][k].wait_recv()
                row = (ALL, at(s, 1, -o2), at(s, 2, -o))
                if (j < 2) == (k == 0):
                    onward[i][k].append((cast(s, row, s[2], o), o2))
                relays[i][k].append(relay(s, row))

    un_yx.wait_recv()
    un_relay.append(un_send((c, ALL, 1 - xl, ALL, left), sibling))
    for o, cp in zip((1, 3, 2), un_xy):
        cp.wait_recv()
        un_relay.append(un_send((c, (y + 4 - o) % 4, ALL, ALL, right), sibling))

    for k, o in enumerate((1, 3)):
        for i, s in enumerate(SHARES):
            for cp in relays[i][k]:
                cp.wait_recv()
            plane(s, at(s, 2, -o))

    last = [[] for _ in range(n)]
    for k, o in enumerate((1, 3)):
        for i, s in enumerate(SHARES):
            for cp, o2 in onward[i][k]:
                cp.wait_recv()
                last[i].append(relay(s, (ALL, at(s, 1, -o2), at(s, 2, 2))))

    for cp in un_relay:
        cp.wait_recv()
    for h in range(2):
        b = UN[h].reshape(256, HALF)
        part = lax.dot_general(b, A[h], NT, preferred_element_type=F32)
        norm = fold(b)
        if h:
            part = part + DU[...]
            norm = norm + un_norm
            norm = jnp.sum(norm, axis=1, keepdims=True)
            near = jnp.min(norm - 2.0 * part, axis=0, keepdims=True)
        else:
            DU[...] = part
            un_norm = norm

    for i, s in enumerate(SHARES):
        for cp in last[i]:
            cp.wait_recv()
        plane(s, at(s, 2, 2))

    def smallest(dots, norms):
        total = jnp.sum(norms.reshape(-1, 128), axis=1, keepdims=True)
        return jnp.min(total - 2.0 * dots.reshape(-1, ROWS), axis=0, keepdims=True)

    best = jnp.full((1, ROWS), jnp.inf, F32)
    for i in range(4):
        best = jnp.minimum(best, smallest(D[i], NRM[i]))
    for i in range(2):
        px = x - xl + i
        near = jnp.minimum(near, smallest(D[px, :, z], NRM[px, :, z]))
    base = AN[0:1, :]
    near_ref[...] = base + near
    final_ref[...] = base + best
    for cp in sent:
        cp.wait_send()


def body(candidates, round_one, counts, chosen):
    copies = 200
    vmem = pltpu.VMEM
    near, final = pl.pallas_call(
        kernel,
        out_shape=(jax.ShapeDtypeStruct((1, ROWS), F32), jax.ShapeDtypeStruct((1, ROWS), F32)),
        in_specs=[
            pl.BlockSpec(memory_space=pl.ANY),
            pl.BlockSpec(memory_space=pl.ANY),
            pl.BlockSpec(memory_space=vmem),
            pl.BlockSpec(memory_space=vmem),
        ],
        out_specs=(pl.BlockSpec(memory_space=vmem), pl.BlockSpec(memory_space=vmem)),
        scratch_shapes=[
            vmem((2, ROWS, HALF), BF16),
            vmem((2, SLOTS, HALF), BF16),
            vmem((16, 8, 128), jnp.int32),
            vmem((CHIPS, 16, HALF), BF16),
            vmem((CHIPS, 16, HALF), BF16),
            vmem((CHIPS, 16, HALF), BF16),
            vmem((CHIPS, 16, HALF), BF16),
            vmem((2, 4, 4, 4, SHARE, HALF), BF16),
            vmem((2, 4, 2, REST, HALF), BF16),
            vmem((4, 4, 4, SHARE, ROWS), F32),
            vmem((4, 4, 4, SHARE, 128), F32),
            vmem((256, ROWS), F32),
            vmem((1, ROWS), F32),
            pltpu.SemaphoreType.DMA((3,)),
            pltpu.SemaphoreType.DMA((copies,)),
            pltpu.SemaphoreType.DMA((copies,)),
        ],
        compiler_params=pltpu.CompilerParams(
            collective_id=0, has_side_effects=True, vmem_limit_bytes=56 << 20),
    )(candidates, round_one, counts, chosen)
    return near.reshape(ROWS), final.reshape(ROWS)


def solution(mesh):
    in_specs = (P(("grp", "mem"), None), P(("grp", "mem"), None), P("grp", "mem"), P("grp", None))
    out_specs = (P(("grp", "mem")), P(("grp", "mem")))
    return jax.shard_map(body, mesh=mesh, in_specs=in_specs, out_specs=out_specs, check_vma=False)
```

```python
import jax
import jax.numpy as jnp
from jax import lax
from jax.experimental import pallas as pl
from jax.experimental.pallas import tpu as pltpu
from jax.sharding import PartitionSpec as P

MESH = pl.DeviceIdType.MESH
NT = (((1,), (1,)), ((), ()))
F32 = jnp.float32
BF16 = jnp.bfloat16
ALL = slice(None)

ROWS = 1024
WIDTH = 4096
HALF = WIDTH // 2
SLOTS = 64
PICKS = 128
CHIPS = 8
SHARE = PICKS // CHIPS
REST = 32
CUT = HALF // 2

SHARES = (
    (1, 0, 2, 0, 896),
    (0, 2, 1, 896, 1408),
    (1, 2, 0, 1408, 2048),
)


def place():
    g, m = lax.axis_index("grp"), lax.axis_index("mem")
    x = (g // 4) * 2 + (m // 2) % 2
    return x, m // 4, g % 4, m % 2


def device(x, y, z, c):
    return {"grp": (x // 2) * 4 + z, "mem": y * 4 + (x % 2) * 2 + c}


def fold(b):
    b = b.astype(F32)
    b = b * b
    total = b[:, 0:128]
    for k in range(128, b.shape[1], 128):
        total = total + b[:, k:k + 128]
    return total


def kernel(
    cand_ref, slot_ref, count_ref, chosen_ref, out_ref,
    A, S, CN, M, R, MO, RO, FIN, UN, D, NRM, DU,
    local_sem, send_sem, recv_sem,
):
    x, y, z, c = place()
    pos3 = (x, y, z)
    xl = x % 2
    other = 1 - c
    me = lax.axis_index("mem")
    chip = y * 2 + xl
    sibling = device(x, y, z, other)
    used = {"send": 0, "recv": 0}

    def fresh(kind):
        used[kind] += 1
        return used[kind] - 1

    def send(src, dst, dev, out, into):
        pltpu.make_async_remote_copy(
            src_ref=src, dst_ref=dst, send_sem=send_sem.at[out], recv_sem=recv_sem.at[into],
            device_id=dev, device_id_type=MESH,
        ).start()

    def span(ref, out, into):
        return pltpu.make_async_remote_copy(
            src_ref=ref, dst_ref=ref, send_sem=send_sem.at[out], recv_sem=recv_sem.at[into],
            device_id=sibling, device_id_type=MESH,
        )

    def arrived(ref, into):
        span(ref, 0, into).wait_recv()

    leaving = []

    def leave(ref, out):
        leaving.append((ref, out))

    def device_at(dim, coord):
        p = list(pos3)
        p[dim] = coord
        return device(p[0], p[1], p[2], c)

    def in_group(dy, dx, dc):
        return device(x - xl + (xl + dx) % 2, (y + dy) % 4, z, (c + dc) % 2)

    partner, outer = x - xl + 1 - xl, (x + 4 - 1 + 2 * xl) % 4

    def neighbours(dim):
        if dim == 0:
            return ((partner, partner), (outer, outer))
        p = pos3[dim]
        return (((p + 1) % 4, (p + 3) % 4), ((p + 3) % 4, (p + 1) % 4))

    def far(dim):
        return (pos3[dim] + 2) % 4

    mine = pltpu.make_async_copy(
        slot_ref.at[:, pl.ds(pl.multiple_of(c * HALF, HALF), HALF)], S.at[c], local_sem.at[0])
    mine.start()
    loads = []
    for h in range(2):
        cp = pltpu.make_async_copy(cand_ref.at[:, h * HALF:(h + 1) * HALF], A.at[h], local_sem.at[1 + h])
        cp.start()
        loads.append(cp)

    group_peers = [(dy, dx, dc) for dy in range(4) for dx in range(2) for dc in range(2) if dy or dx or dc]
    partners = [in_group(*o) for o in group_peers]
    partners += [device_at(2, (z + o) % 4) for o in (1, 2, 3)]
    partners += [device_at(0, outer), device_at(0, far(0))]
    barrier = pltpu.get_barrier_semaphore()
    for dev in partners:
        pl.semaphore_signal(barrier, inc=1, device_id=dev, device_id_type=MESH)
    CN[me] = jnp.broadcast_to(count_ref[...], (8, 128))
    pl.semaphore_wait(barrier, len(partners))

    out_counts, in_counts = fresh("send"), fresh("recv")
    for o in group_peers:
        send(CN.at[me], CN.at[me], in_group(*o), out_counts, in_counts)
    leave(CN.at[0:15], out_counts)
    out_slots, in_slots = fresh("send"), fresh("recv")
    send(
        slot_ref.at[:, pl.ds(pl.multiple_of(other * HALF, HALF), HALF)], S.at[c], sibling,
        out_slots, in_slots)
    leave(S.at[0], out_slots)

    D[...] = jnp.zeros_like(D)
    NRM[...] = jnp.zeros_like(NRM)

    lane = lax.broadcasted_iota(jnp.int32, (1, 128), 1)
    row8 = lax.broadcasted_iota(jnp.int32, (8, 128), 0)
    row16 = lax.broadcasted_iota(jnp.int32, (16, 128), 0)
    row128 = lax.broadcasted_iota(jnp.int32, (128, 128), 0)
    chosen_col = jnp.transpose(jnp.broadcast_to(chosen_ref[...].astype(F32), (128, 128)))

    def below(p):
        return whole(jnp.sum(jnp.where(chosen_col < p, 1.0, 0.0), axis=0, keepdims=True))

    def whole(v):
        return v.astype(jnp.int32)

    def hot(rows, key):
        return jnp.where(rows == key, 1.0, 0.0).astype(BF16)

    arrived(CN.at[0:15], in_counts)
    cnt = jnp.max(CN[...].astype(F32), axis=1)
    off = jnp.zeros((16, 128), F32)
    for m in range(15):
        off = off + jnp.where(row16 > m, cnt[m:m + 1, :], 0.0)
    end = off + cnt

    def pick(table, index):
        return jnp.sum(jnp.where(row16 == index, table, 0.0), axis=0, keepdims=True)

    def amount(lo, hi, goal):
        return (hi - lo - (goal - lo + 1024) % 8 + 7) // 8

    first_off, last_end = pick(off, 2 * chip), pick(end, 2 * chip + 1)
    second = lane >= SLOTS
    within = lane % SLOTS
    spot = jnp.where(second, pick(off, 2 * chip + 1), first_off) + within.astype(F32)
    live = jnp.where(second, pick(cnt, 2 * chip + 1), pick(cnt, 2 * chip))
    alive = within.astype(F32) < live
    is_chosen = jnp.sum(jnp.where(chosen_col == spot, 1.0, 0.0), axis=0, keepdims=True) > 0.5
    q, q0, q1 = below(spot), below(first_off), below(last_end)
    u, u0 = whole(spot) - q, whole(first_off) - q0
    rank, nth = (u - u0) // 8, 15 - (u - u0) // 8
    apart = nth < amount(q0, q1, u % 8)
    key = jnp.where(is_chosen, (q % 8) * 16 + (q - q0) // 8, jnp.where(apart, -1, (u % 8) * 16 + nth))
    key_apart = jnp.where(is_chosen, -1, jnp.where(apart, u % 8, -1))
    hot_main = hot(row128, jnp.where(alive, key, -1))
    hot_apart = hot(row8, jnp.where(alive, key_apart, -1))

    mine.wait()
    arrived(S.at[0], in_slots)
    held = S[...].reshape(2 * SLOTS, HALF)
    M[...] = jnp.dot(hot_main, held, preferred_element_type=F32).astype(BF16).reshape(CHIPS, 16, HALF)
    out_swap, in_swap = fresh("send"), fresh("recv")
    chip_peers = [(dy, dx) for dy in range(4) for dx in range(2) if dy or dx]

    def target(dy, dx):
        return (y + dy) % 4 * 2 + (xl + dx) % 2

    for o in chip_peers:
        send(M.at[target(*o)], R.at[chip], in_group(*o, 0), out_swap, in_swap)
    leave(M.at[0:7], out_swap)
    MO[...] = jnp.dot(hot_apart, held, preferred_element_type=F32).reshape(CHIPS, 1, HALF)
    out_apart, in_apart = fresh("send"), fresh("recv")
    for o in chip_peers:
        send(MO.at[target(*o)], RO.at[chip], in_group(*o, 0), out_apart, in_apart)
    leave(MO.at[0:7], out_apart)
    R[chip] = M[chip]
    RO[chip] = MO[chip]

    def bounds(source):
        low = jnp.sum(jnp.where(row16 == 2 * source, off, 0.0), axis=0, keepdims=True)
        high = jnp.sum(jnp.where(row16 == 2 * source + 1, end, 0.0), axis=0, keepdims=True)
        ql, qh = below(low), below(high)
        return ql, qh, whole(low) - ql, whole(high) - qh

    ql, qh, ul, uh = bounds(lane // 16)
    nth = lane % 16
    at_q = ql + (chip - ql + 1024) % 8 + 8 * nth
    at_u = ul + (chip - ul + 1024) % 8 + 8 * (15 - nth)
    fits = nth >= amount(ql, qh, chip)
    row32 = lax.broadcasted_iota(jnp.int32, (REST, 128), 0)
    take_chosen = hot(row16, jnp.where(at_q < qh, at_q // 8, -1))
    take_rest = hot(row32, jnp.where(fits, jnp.where(at_u < uh, at_u // 8, -1), -1))
    ql, qh, ul, uh = bounds(lane)
    total = amount(ul, uh, chip)
    excess = amount(ql, qh, chip) + total > 16
    at_u = ul + (chip - ul + 1024) % 8 + 8 * (total - 1)
    take_apart = hot(row32, jnp.where(lane < CHIPS, jnp.where(excess, at_u // 8, -1), -1))

    for cp in loads:
        cp.wait()
    for i in range(8):
        rows = slice(i * 128, (i + 1) * 128)
        part = fold(A[0, rows, :]) + fold(A[1, rows, :])
        out_ref[2:3, rows] = jnp.sum(jnp.transpose(part), axis=0, keepdims=True)

    arrived(R.at[0:7], in_swap)
    got = R[...].reshape(CHIPS * 16, HALF)
    FIN[c, x, y, z] = jnp.dot(take_chosen, got, preferred_element_type=F32).astype(BF16)

    def block(share, s1, s2, s3, half=None):
        d1, d2, d3, lo, hi = share
        sel = [None] * 3
        sel[d1], sel[d2], sel[d3] = s1, s2, s3
        return FIN.at[(c if half is None else half, *sel, ALL, slice(lo, hi))]

    def blocks(share, *shape):
        lead = [slice(0, k) for k in shape]
        lead = [0] * (4 - len(lead)) + lead
        return FIN.at[(*lead, ALL, slice(share[3], share[4]))]

    n = len(SHARES)
    own = [tuple(pos3[s[k]] for k in range(3)) for s in SHARES]
    outs = [[fresh("send") for _ in range(3)] for _ in range(n)]
    planes_in = [[fresh("recv") for _ in range(4)] for _ in range(n)]
    for i, s in enumerate(SHARES):
        leave(blocks(s, 2, 3), outs[i][0])
        leave(blocks(s, 2, 4, 3), outs[i][1])
        leave(blocks(s, 2, 4, 4, 3), outs[i][2])
    out_own = fresh("send")

    def cast(i, k, index, coord, into):
        s = SHARES[i]
        ref = block(s, *index)
        send(ref, ref, device_at(s[k], coord), outs[i][k], into)

    def relay(i, k, index, plane):
        ref = block(SHARES[i], *index)
        send(ref, ref, sibling, outs[i][k], planes_in[i][plane])

    first_in = [fresh("recv") for _ in range(n)]
    for i, s in enumerate(SHARES):
        for o in (1, 3, 2):
            cast(i, 0, own[i], (own[i][0] + o) % 4, first_in[i])
        ref = block(s, *own[i])
        send(ref, ref, sibling, out_own, planes_in[i][0])
    leave(FIN.at[0, 0, 0, 0], out_own)

    rest = jnp.dot(take_rest, got, preferred_element_type=F32)
    arrived(RO.at[0:7], in_apart)
    lone = RO[...].reshape(CHIPS, HALF).astype(BF16)
    lone = jnp.concatenate([lone, jnp.zeros((128 - CHIPS, HALF), BF16)], axis=0)
    rest = rest + jnp.dot(take_apart, lone, preferred_element_type=F32)
    UN[c, y, xl] = rest.astype(BF16)
    left, right = slice(0, CUT), slice(CUT, HALF)
    un_in = fresh("recv")
    un_out = fresh("send")
    leave(UN.at[0], un_out)
    outs_y, ins_y = fresh("send"), fresh("recv")
    outs_x, ins_x = fresh("send"), fresh("recv")
    outs_yx, ins_yx = fresh("send"), fresh("recv")
    outs_xy, ins_xy = fresh("send"), fresh("recv")

    def pass_on(sel, dev, out, into):
        ref = UN.at[sel]
        send(ref, ref, dev, out, into)

    for o in (1, 3, 2):
        pass_on((c, y, xl, ALL, left), in_group(o, 0, 0), outs_y, ins_y)
    leave(UN.at[0, 0:3, 0, :, left], outs_y)
    pass_on((c, y, xl, ALL, right), in_group(0, 1, 0), outs_x, ins_x)
    leave(UN.at[0, 0, 0, :, right], outs_x)
    pass_on((c, y, xl), sibling, un_out, un_in)

    line_in = [[[fresh("recv") for _ in range(2)] for _ in range(4)] for _ in range(n)]
    lines = [[None] * 4 for _ in range(n)]
    second_in = [[fresh("recv") for _ in range(3)] for _ in range(n)]

    def third(i, j, coord):
        s = SHARES[i]
        lines[i][j] = coord
        for k, (goal, _) in enumerate(neighbours(s[2])):
            cast(i, 2, (ALL, coord, own[i][2]), goal, line_in[i][j][k])

    for i, s in enumerate(SHARES):
        arrived(blocks(s, 3), first_in[i])
        row = (ALL, own[i][1], own[i][2])
        for k, (goal, _) in enumerate(neighbours(s[1])):
            cast(i, 1, row, goal, second_in[i][k])
        if s[1] != 0:
            cast(i, 1, row, far(s[1]), second_in[i][2])
        third(i, 0, own[i][1])
        for o in (1, 3, 2):
            relay(i, 0, ((own[i][0] + o) % 4, own[i][1], own[i][2]), 0)

    arrived(UN.at[0, 0, 0, :, right], ins_x)
    for o in (1, 3, 2):
        pass_on((c, y, ALL, ALL, right), in_group(o, 0, 0), outs_xy, ins_xy)
    leave(UN.at[0, 0:3, :, :, right], outs_xy)
    pass_on((c, y, 1 - xl, ALL, right), sibling, un_out, un_in)
    arrived(UN.at[0, 0:3, 0, :, left], ins_y)
    pass_on((c, ALL, xl, ALL, left), in_group(0, 1, 0), outs_yx, ins_yx)
    leave(UN.at[0, :, 0, :, left], outs_yx)
    for o in (1, 2, 3):
        pass_on((c, (y + o) % 4, xl, ALL, left), sibling, un_out, un_in)

    for j in range(3):
        for i, s in enumerate(SHARES):
            arrived(blocks(s, 4), second_in[i][j])
            coord = neighbours(s[1])[j][1] if j < 2 else far(s[1])
            row = (ALL, coord, own[i][2])
            if s[1] == 0 and j == 0:
                cast(i, 1, row, outer, second_in[i][2])
            third(i, 1 + j, coord)
            relay(i, 1, row, 0)

    arrived(UN.at[0, :, 0, :, left], ins_yx)
    pass_on((c, ALL, 1 - xl, ALL, left), sibling, un_out, un_in)
    arrived(UN.at[0, 0:3, :, :, right], ins_xy)
    for o in (1, 2, 3):
        pass_on((c, (y + o) % 4, ALL, ALL, right), sibling, un_out, un_in)

    def plane(i, p):
        d3, lo, hi = SHARES[i][2:]
        where = [ALL, ALL, ALL, ALL]
        where[d3] = p
        where = tuple(where)
        total = D[where + (ALL,)].reshape(256, ROWS)
        norm = NRM[where + (ALL,)].reshape(256, 128)
        for h in range(2):
            b = FIN[(h,) + where + (slice(lo, hi),)].reshape(256, hi - lo)
            total = total + lax.dot_general(b, A[h, :, lo:hi], NT, preferred_element_type=F32)
            norm = norm + fold(b)
        D[where + (ALL,)] = total.reshape(4, 4, SHARE, ROWS)
        NRM[where + (ALL,)] = norm.reshape(4, 4, SHARE, 128)

    far_in = [[fresh("recv") for _ in range(4)] for _ in range(n)]
    for j in range(4):
        for i, s in enumerate(SHARES):
            near_by = neighbours(s[2])
            for k, (goal, origin) in enumerate(near_by):
                arrived(blocks(s, 4), line_in[i][j][k])
                row = (ALL, lines[i][j], origin)
                if s[2] == 0:
                    if k == 0:
                        cast(i, 2, row, outer, far_in[i][j])
                elif (j < 2) == (k == 0):
                    cast(i, 2, row, goal, far_in[i][j])
                relay(i, 2, row, 1 + k)
        if j < n:
            arrived(blocks(SHARES[j], 4, 4), planes_in[j][0])
            plane(j, own[j][2])

    arrived(UN.at[0], un_in)
    un_norm = 0.0
    for h in range(2):
        b = UN[h].reshape(256, HALF)
        part = lax.dot_general(b, A[h], NT, preferred_element_type=F32)
        un_norm = un_norm + fold(b)
        if h:
            un_norm = jnp.sum(un_norm, axis=1, keepdims=True)
            out_ref[0:1, :] = jnp.min(un_norm - 2.0 * (DU[...] + part), axis=0, keepdims=True)
        else:
            DU[...] = part

    def far_line(j):
        for i, s in enumerate(SHARES):
            arrived(blocks(s, 4), far_in[i][j])
            relay(i, 2, (ALL, lines[i][j], far(s[2])), 3)

    j = 0
    for k in range(2):
        for i, s in enumerate(SHARES):
            arrived(blocks(s, 4, 4), planes_in[i][1 + k])
            plane(i, neighbours(s[2])[k][1])
            if 1 <= k * n + i <= 4:
                far_line(j)
                j += 1
    for i, s in enumerate(SHARES):
        arrived(blocks(s, 4, 4), planes_in[i][3])
        plane(i, far(s[2]))

    def smallest(dots, norms):
        total = jnp.sum(norms.reshape(-1, 128), axis=1, keepdims=True)
        return jnp.min(total - 2.0 * dots.reshape(-1, ROWS), axis=0, keepdims=True)

    best = jnp.full((1, ROWS), jnp.inf, F32)
    for i in range(4):
        best = jnp.minimum(best, smallest(D[i], NRM[i]))
    near = out_ref[0:1, :]
    for i in range(2):
        px = x - xl + i
        near = jnp.minimum(near, smallest(D[px, :, z], NRM[px, :, z]))
    out_ref[0:1, :] = near
    out_ref[1:2, :] = best
    for ref, out in leaving:
        span(ref, out, 0).wait_send()


def body(candidates, round_one, counts, chosen):
    vmem = pltpu.VMEM
    out = pl.pallas_call(
        kernel,
        out_shape=jax.ShapeDtypeStruct((3, ROWS), F32),
        in_specs=[
            pl.BlockSpec(memory_space=pl.ANY),
            pl.BlockSpec(memory_space=pl.ANY),
            pl.BlockSpec(memory_space=vmem),
            pl.BlockSpec(memory_space=vmem),
        ],
        out_specs=pl.BlockSpec(memory_space=vmem),
        scratch_shapes=[
            vmem((2, ROWS, HALF), BF16),
            vmem((2, SLOTS, HALF), BF16),
            vmem((16, 8, 128), jnp.int32),
            vmem((CHIPS, 16, HALF), BF16),
            vmem((CHIPS, 16, HALF), BF16),
            vmem((CHIPS, 1, HALF), F32),
            vmem((CHIPS, 1, HALF), F32),
            vmem((2, 4, 4, 4, SHARE, HALF), BF16),
            vmem((2, 4, 2, REST, HALF), BF16),
            vmem((4, 4, 4, SHARE, ROWS), F32),
            vmem((4, 4, 4, SHARE, 128), F32),
            vmem((256, ROWS), F32),
            pltpu.SemaphoreType.DMA((3,)),
            pltpu.SemaphoreType.DMA((19,)),
            pltpu.SemaphoreType.DMA((69,)),
        ],
        compiler_params=pltpu.CompilerParams(
            collective_id=0, has_side_effects=True, vmem_limit_bytes=56 << 20),
    )(candidates, round_one, counts, chosen)
    return out[0] + out[2], out[1] + out[2]


def solution(mesh):
    in_specs = (P(("grp", "mem"), None), P(("grp", "mem"), None), P("grp", "mem"), P("grp", None))
    out_specs = (P(("grp", "mem")), P(("grp", "mem")))
    return jax.shard_map(body, mesh=mesh, in_specs=in_specs, out_specs=out_specs, check_vma=False)
```

```python
import jax
import jax.numpy as jnp
from jax import lax
from jax.experimental import pallas as pl
from jax.experimental.pallas import tpu as pltpu
from jax.sharding import PartitionSpec as P

MESH = pl.DeviceIdType.MESH
NT = (((1,), (1,)), ((), ()))
F32 = jnp.float32
BF16 = jnp.bfloat16
ALL = slice(None)

ROWS = 1024
WIDTH = 4096
HALF = WIDTH // 2
SLOTS = 64
PICKS = 128
CHIPS = 8
SHARE = PICKS // CHIPS
REST = 32
CUT = HALF * 3 // 4

SHARES = (
    (1, 0, 2, 0, 1024),
    (0, 2, 1, 1024, 1536),
    (2, 1, 0, 1536, 2048),
)


def place():
    g, m = lax.axis_index("grp"), lax.axis_index("mem")
    x = (g // 4) * 2 + (m // 2) % 2
    return x, m // 4, g % 4, m % 2


def device(x, y, z, c):
    return {"grp": (x // 2) * 4 + z, "mem": y * 4 + (x % 2) * 2 + c}


def fold(b):
    b = b.astype(F32)
    b = b * b
    total = b[:, 0:128]
    for k in range(128, b.shape[1], 128):
        total = total + b[:, k:k + 128]
    return total


def kernel(
    cand_ref, slot_ref, count_ref, chosen_ref, out_ref,
    CT, CH, A, S, CN, M, R, MO, RO, FIN, UN, D, NRM, DU, NU,
    local_sem, send_sem, recv_sem,
):
    x, y, z, c = place()
    pos3 = (x, y, z)
    xl = x % 2
    other = 1 - c
    me = lax.axis_index("mem")
    chip = y * 2 + xl
    sibling = device(x, y, z, other)
    used = {"send": 0, "recv": 0}

    def fresh(kind):
        used[kind] += 1
        return used[kind] - 1

    def send(src, dst, dev, out, into):
        pltpu.make_async_remote_copy(
            src_ref=src, dst_ref=dst, send_sem=send_sem.at[out], recv_sem=recv_sem.at[into],
            device_id=dev, device_id_type=MESH,
        ).start()

    def span(ref, out, into):
        return pltpu.make_async_remote_copy(
            src_ref=ref, dst_ref=ref, send_sem=send_sem.at[out], recv_sem=recv_sem.at[into],
            device_id=sibling, device_id_type=MESH,
        )

    def arrived(ref, into):
        span(ref, 0, into).wait_recv()

    leaving = []

    def leave(ref, out):
        leaving.append((ref, out))

    def device_at(dim, coord):
        p = list(pos3)
        p[dim] = coord
        return device(p[0], p[1], p[2], c)

    def in_group(dy, dx, dc):
        return device(x - xl + (xl + dx) % 2, (y + dy) % 4, z, (c + dc) % 2)

    partner, outer = x - xl + 1 - xl, (x + 4 - 1 + 2 * xl) % 4

    def neighbours(dim):
        if dim == 0:
            return ((partner, partner), (outer, outer))
        p = pos3[dim]
        return (((p + 1) % 4, (p + 3) % 4), ((p + 3) % 4, (p + 1) % 4))

    def far(dim):
        return (pos3[dim] + 2) % 4

    group_peers = [(dy, dx, dc) for dy in range(4) for dx in range(2) for dc in range(2) if dy or dx or dc]
    partners = [in_group(*o) for o in group_peers]
    partners += [device_at(2, (z + o) % 4) for o in (1, 2, 3)]
    partners += [device_at(0, outer), device_at(0, far(0))]
    barrier = pltpu.get_barrier_semaphore()
    for dev in partners:
        pl.semaphore_signal(barrier, inc=1, device_id=dev, device_id_type=MESH)
    small = [
        pltpu.make_async_copy(count_ref, CT, local_sem.at[3]),
        pltpu.make_async_copy(chosen_ref, CH, local_sem.at[4]),
    ]
    for cp in small:
        cp.start()
    mine = pltpu.make_async_copy(
        slot_ref.at[:, pl.ds(pl.multiple_of(c * HALF, HALF), HALF)], S.at[c], local_sem.at[0])
    mine.start()
    loads = []
    for h in range(2):
        cp = pltpu.make_async_copy(cand_ref.at[:, h * HALF:(h + 1) * HALF], A.at[h], local_sem.at[1 + h])
        cp.start()
        loads.append(cp)

    for cp in small:
        cp.wait()
    CN[me] = jnp.broadcast_to(CT[...], (8, 128))
    pl.semaphore_wait(barrier, len(partners))

    out_counts, in_counts = fresh("send"), fresh("recv")
    for o in group_peers:
        send(CN.at[me], CN.at[me], in_group(*o), out_counts, in_counts)
    leave(CN.at[0:15], out_counts)
    out_slots, in_slots = fresh("send"), fresh("recv")
    send(
        slot_ref.at[:, pl.ds(pl.multiple_of(other * HALF, HALF), HALF)], S.at[c], sibling,
        out_slots, in_slots)
    leave(S.at[0], out_slots)

    D[...] = jnp.zeros_like(D)
    NRM[...] = jnp.zeros_like(NRM)

    lane = lax.broadcasted_iota(jnp.int32, (1, 128), 1)
    row8 = lax.broadcasted_iota(jnp.int32, (8, 128), 0)
    row16 = lax.broadcasted_iota(jnp.int32, (16, 128), 0)
    row128 = lax.broadcasted_iota(jnp.int32, (128, 128), 0)
    chosen_col = jnp.transpose(jnp.broadcast_to(CH[...].astype(F32), (128, 128)))

    def below(p):
        return whole(jnp.sum(jnp.where(chosen_col < p, 1.0, 0.0), axis=0, keepdims=True))

    def whole(v):
        return v.astype(jnp.int32)

    def hot(rows, key):
        return jnp.where(rows == key, 1.0, 0.0).astype(BF16)

    arrived(CN.at[0:15], in_counts)
    cnt = jnp.max(CN[...].astype(F32), axis=1)
    off = jnp.zeros((16, 128), F32)
    for m in range(15):
        off = off + jnp.where(row16 > m, cnt[m:m + 1, :], 0.0)
    end = off + cnt

    def pick(table, index):
        return jnp.sum(jnp.where(row16 == index, table, 0.0), axis=0, keepdims=True)

    def amount(lo, hi, goal):
        return (hi - lo - (goal - lo + 1024) % 8 + 7) // 8

    first_off, last_end = pick(off, 2 * chip), pick(end, 2 * chip + 1)
    second = lane >= SLOTS
    within = lane % SLOTS
    spot = jnp.where(second, pick(off, 2 * chip + 1), first_off) + within.astype(F32)
    live = jnp.where(second, pick(cnt, 2 * chip + 1), pick(cnt, 2 * chip))
    alive = within.astype(F32) < live
    is_chosen = jnp.sum(jnp.where(chosen_col == spot, 1.0, 0.0), axis=0, keepdims=True) > 0.5
    q, q0, q1 = below(spot), below(first_off), below(last_end)
    u, u0 = whole(spot) - q, whole(first_off) - q0
    rank, nth = (u - u0) // 8, 15 - (u - u0) // 8
    apart = nth < amount(q0, q1, u % 8)
    key = jnp.where(is_chosen, (q % 8) * 16 + (q - q0) // 8, jnp.where(apart, -1, (u % 8) * 16 + nth))
    key_apart = jnp.where(is_chosen, -1, jnp.where(apart, u % 8, -1))
    hot_main = hot(row128, jnp.where(alive, key, -1))
    hot_apart = hot(row8, jnp.where(alive, key_apart, -1))

    mine.wait()
    arrived(S.at[0], in_slots)
    held = S[...].reshape(2 * SLOTS, HALF)
    M[...] = jnp.dot(hot_main, held, preferred_element_type=F32).astype(BF16).reshape(CHIPS, 16, HALF)
    out_swap, in_swap = fresh("send"), fresh("recv")
    chip_peers = [(dy, dx) for dy in range(4) for dx in range(2) if dy or dx]

    def target(dy, dx):
        return (y + dy) % 4 * 2 + (xl + dx) % 2

    for o in chip_peers:
        send(M.at[target(*o)], R.at[chip], in_group(*o, 0), out_swap, in_swap)
    leave(M.at[0:7], out_swap)
    MO[...] = jnp.dot(hot_apart, held, preferred_element_type=F32).reshape(CHIPS, 1, HALF)
    out_apart, in_apart = fresh("send"), fresh("recv")
    for o in chip_peers:
        send(MO.at[target(*o)], RO.at[chip], in_group(*o, 0), out_apart, in_apart)
    leave(MO.at[0:7], out_apart)
    R[chip] = M[chip]
    RO[chip] = MO[chip]

    def bounds(source):
        low = jnp.sum(jnp.where(row16 == 2 * source, off, 0.0), axis=0, keepdims=True)
        high = jnp.sum(jnp.where(row16 == 2 * source + 1, end, 0.0), axis=0, keepdims=True)
        ql, qh = below(low), below(high)
        return ql, qh, whole(low) - ql, whole(high) - qh

    ql, qh, ul, uh = bounds(lane // 16)
    nth = lane % 16
    at_q = ql + (chip - ql + 1024) % 8 + 8 * nth
    at_u = ul + (chip - ul + 1024) % 8 + 8 * (15 - nth)
    fits = nth >= amount(ql, qh, chip)
    row32 = lax.broadcasted_iota(jnp.int32, (REST, 128), 0)
    take_chosen = hot(row16, jnp.where(at_q < qh, at_q // 8, -1))
    take_rest = hot(row32, jnp.where(fits, jnp.where(at_u < uh, at_u // 8, -1), -1))
    ql, qh, ul, uh = bounds(lane)
    total = amount(ul, uh, chip)
    excess = amount(ql, qh, chip) + total > 16
    at_u = ul + (chip - ul + 1024) % 8 + 8 * (total - 1)
    take_apart = hot(row32, jnp.where(lane < CHIPS, jnp.where(excess, at_u // 8, -1), -1))

    for cp in loads:
        cp.wait()
    for i in range(8):
        rows = slice(i * 128, (i + 1) * 128)
        part = fold(A[0, rows, :]) + fold(A[1, rows, :])
        out_ref[2:3, rows] = jnp.sum(jnp.transpose(part), axis=0, keepdims=True)

    arrived(R.at[0:7], in_swap)
    got = R[...].reshape(CHIPS * 16, HALF)
    FIN[c, x, y, z] = jnp.dot(take_chosen, got, preferred_element_type=F32).astype(BF16)

    def block(share, s1, s2, s3, half=None):
        d1, d2, d3, lo, hi = share
        sel = [None] * 3
        sel[d1], sel[d2], sel[d3] = s1, s2, s3
        return FIN.at[(c if half is None else half, *sel, ALL, slice(lo, hi))]

    def blocks(share, *shape):
        lead = [slice(0, k) for k in shape]
        lead = [0] * (4 - len(lead)) + lead
        return FIN.at[(*lead, ALL, slice(share[3], share[4]))]

    n = len(SHARES)
    own = [tuple(pos3[s[k]] for k in range(3)) for s in SHARES]
    outs = [[fresh("send") for _ in range(3)] for _ in range(n)]
    planes_in = [[fresh("recv") for _ in range(4)] for _ in range(n)]
    for i, s in enumerate(SHARES):
        leave(blocks(s, 2, 3), outs[i][0])
        leave(blocks(s, 2, 4, 3), outs[i][1])
        leave(blocks(s, 2, 4, 4, 3), outs[i][2])
    out_own = fresh("send")

    def cast(i, k, index, coord, into):
        s = SHARES[i]
        ref = block(s, *index)
        send(ref, ref, device_at(s[k], coord), outs[i][k], into)

    def relay(i, k, index, plane):
        ref = block(SHARES[i], *index)
        send(ref, ref, sibling, outs[i][k], planes_in[i][plane])

    first_in = [fresh("recv") for _ in range(n)]
    for i, s in enumerate(SHARES):
        for o in (1, 3, 2):
            cast(i, 0, own[i], (own[i][0] + o) % 4, first_in[i])
        ref = block(s, *own[i])
        send(ref, ref, sibling, out_own, planes_in[i][0])
    leave(FIN.at[0, 0, 0, 0], out_own)

    rest = jnp.dot(take_rest, got, preferred_element_type=F32)
    arrived(RO.at[0:7], in_apart)
    lone = RO[...].reshape(CHIPS, HALF).astype(BF16)
    lone = jnp.concatenate([lone, jnp.zeros((128 - CHIPS, HALF), BF16)], axis=0)
    rest = rest + jnp.dot(take_apart, lone, preferred_element_type=F32)
    UN[c, y, xl] = rest.astype(BF16)
    left, right = slice(0, CUT), slice(CUT, HALF)
    un_in = fresh("recv")
    un_out = fresh("send")
    leave(UN.at[0], un_out)
    outs_y, ins_y = fresh("send"), fresh("recv")
    outs_x, ins_x = fresh("send"), fresh("recv")
    outs_yx, ins_yx = fresh("send"), fresh("recv")
    outs_xy, ins_xy = fresh("send"), fresh("recv")

    def pass_on(sel, dev, out, into):
        ref = UN.at[sel]
        send(ref, ref, dev, out, into)

    for o in (1, 3, 2):
        pass_on((c, y, xl, ALL, left), in_group(o, 0, 0), outs_y, ins_y)
    leave(UN.at[0, 0:3, 0, :, left], outs_y)
    pass_on((c, y, xl, ALL, right), in_group(0, 1, 0), outs_x, ins_x)
    leave(UN.at[0, 0, 0, :, right], outs_x)
    pass_on((c, y, xl), sibling, un_out, un_in)

    line_in = [[[fresh("recv") for _ in range(2)] for _ in range(4)] for _ in range(n)]
    lines = [[None] * 4 for _ in range(n)]
    second_in = [[fresh("recv") for _ in range(3)] for _ in range(n)]

    def third(i, j, coord):
        s = SHARES[i]
        lines[i][j] = coord
        for k, (goal, _) in enumerate(neighbours(s[2])):
            cast(i, 2, (ALL, coord, own[i][2]), goal, line_in[i][j][k])

    for i in (1, 2, 0):
        s = SHARES[i]
        arrived(blocks(s, 3), first_in[i])
        row = (ALL, own[i][1], own[i][2])
        for k, (goal, _) in enumerate(neighbours(s[1])):
            cast(i, 1, row, goal, second_in[i][k])
        if s[1] != 0:
            cast(i, 1, row, far(s[1]), second_in[i][2])
    for i, s in enumerate(SHARES):
        third(i, 0, own[i][1])
    for i, s in enumerate(SHARES):
        for o in (1, 3, 2):
            relay(i, 0, ((own[i][0] + o) % 4, own[i][1], own[i][2]), 0)

    def more(j):
        for i, s in enumerate(SHARES):
            arrived(blocks(s, 4), second_in[i][j])
            coord = neighbours(s[1])[j][1] if j < 2 else far(s[1])
            row = (ALL, coord, own[i][2])
            if s[1] == 0 and j == 0:
                cast(i, 1, row, outer, second_in[i][2])
            third(i, 1 + j, coord)
            relay(i, 1, row, 0)

    def spread(i, d1, d2, d3):
        sel = [None] * 3
        sel[SHARES[i][0]], sel[SHARES[i][1]], sel[SHARES[i][2]] = d1, d2, d3
        return tuple(sel) + (ALL,)

    def multiply(i, h, parts):
        lo, hi = SHARES[i][3:]
        count = 256 // len(parts)
        rows = [FIN[(h,) + sel + (slice(lo, hi),)].reshape(count, hi - lo) for sel in parts]
        b = rows[0] if len(rows) == 1 else jnp.concatenate(rows, axis=0)
        dots = lax.dot_general(b, A[h, :, lo:hi], NT, preferred_element_type=F32)
        norms = fold(b)
        for p, sel in enumerate(parts):
            at = slice(p * count, (p + 1) * count)
            where = sel + (ALL,)
            D[where] += dots[at].reshape(D[where].shape)
            NRM[where] += norms[at].reshape(NRM[where].shape)

    far_in = [[fresh("recv") for _ in range(4)] for _ in range(n)]

    def line(j):
        for i, s in enumerate(SHARES):
            for k, (goal, origin) in enumerate(neighbours(s[2])):
                arrived(blocks(s, 4), line_in[i][j][k])
                row = (ALL, lines[i][j], origin)
                if s[2] == 0:
                    if k == 0:
                        cast(i, 2, row, outer, far_in[i][j])
                elif (j < 2) == (k == 0):
                    cast(i, 2, row, goal, far_in[i][j])
                relay(i, 2, row, 1 + j // 2)

    def parts(i, k):
        s = SHARES[i]
        if k in (0, 3):
            return [spread(i, ALL, ALL, far(s[2]) if k else own[i][2])]
        js = (0, 1) if k == 1 else (2, 3)
        return [spread(i, ALL, lines[i][j], origin) for j in js for _, origin in neighbours(s[2])]

    def own_half(k):
        for i in (1, 2, 0):
            multiply(i, c, parts(i, k))

    def other_half(k):
        for i in (1, 2, 0):
            arrived(blocks(SHARES[i], 4, 4), planes_in[i][k])
            multiply(i, other, parts(i, k))

    def far_line(j):
        for i in (1, 2, 0):
            s = SHARES[i]
            arrived(blocks(s, 4), far_in[i][j])
            relay(i, 2, (ALL, lines[i][j], far(s[2])), 3)

    def un_dots(h):
        b = UN[h].reshape(256, HALF)
        return lax.dot_general(b, A[h], NT, preferred_element_type=F32), fold(b)

    def un_own():
        DU[...], NU[...] = un_dots(c)

    def un_other():
        arrived(UN.at[0], un_in)
        dots, norms = un_dots(other)
        norms = jnp.sum(NU[...] + norms, axis=1, keepdims=True)
        out_ref[0:1, :] = jnp.min(norms - 2.0 * (DU[...] + dots), axis=0, keepdims=True)

    def un_collect():
        arrived(UN.at[0, :, 0, :, left], ins_yx)
        pass_on((c, ALL, 1 - xl, ALL, left), sibling, un_out, un_in)
        arrived(UN.at[0, 0:3, :, :, right], ins_xy)
        for o in (1, 2, 3):
            pass_on((c, (y + o) % 4, ALL, ALL, right), sibling, un_out, un_in)

    more(0)
    more(1)
    arrived(UN.at[0, 0, 0, :, right], ins_x)
    for o in (1, 3, 2):
        pass_on((c, y, ALL, ALL, right), in_group(o, 0, 0), outs_xy, ins_xy)
    leave(UN.at[0, 0:3, :, :, right], outs_xy)
    pass_on((c, y, 1 - xl, ALL, right), sibling, un_out, un_in)
    arrived(UN.at[0, 0:3, 0, :, left], ins_y)
    pass_on((c, ALL, xl, ALL, left), in_group(0, 1, 0), outs_yx, ins_yx)
    leave(UN.at[0, :, 0, :, left], outs_yx)
    for o in (1, 2, 3):
        pass_on((c, (y + o) % 4, xl, ALL, left), sibling, un_out, un_in)
    line(0)
    more(2)
    own_half(0)
    line(1)
    other_half(0)
    own_half(1)
    line(2)
    other_half(1)
    far_line(0)
    line(3)
    un_collect()
    un_own()
    far_line(1)
    own_half(2)
    far_line(2)
    other_half(2)
    far_line(3)
    un_other()
    own_half(3)
    other_half(3)

    def smallest(dots, norms):
        total = jnp.sum(norms.reshape(-1, 128), axis=1, keepdims=True)
        return jnp.min(total - 2.0 * dots.reshape(-1, ROWS), axis=0, keepdims=True)

    best = jnp.full((1, ROWS), jnp.inf, F32)
    for i in range(4):
        best = jnp.minimum(best, smallest(D[i], NRM[i]))
    near = out_ref[0:1, :]
    for i in range(2):
        px = x - xl + i
        near = jnp.minimum(near, smallest(D[px, :, z], NRM[px, :, z]))
    out_ref[0:1, :] = near
    out_ref[1:2, :] = best
    for ref, out in leaving:
        span(ref, out, 0).wait_send()


def body(candidates, round_one, counts, chosen):
    vmem = pltpu.VMEM
    out = pl.pallas_call(
        kernel,
        out_shape=jax.ShapeDtypeStruct((3, ROWS), F32),
        in_specs=[
            pl.BlockSpec(memory_space=pl.ANY),
            pl.BlockSpec(memory_space=pl.ANY),
            pl.BlockSpec(memory_space=pl.ANY),
            pl.BlockSpec(memory_space=pl.ANY),
        ],
        out_specs=pl.BlockSpec(memory_space=vmem),
        scratch_shapes=[
            vmem((1, 1), jnp.int32),
            vmem((1, PICKS), jnp.int32),
            vmem((2, ROWS, HALF), BF16),
            vmem((2, SLOTS, HALF), BF16),
            vmem((16, 8, 128), jnp.int32),
            vmem((CHIPS, 16, HALF), BF16),
            vmem((CHIPS, 16, HALF), BF16),
            vmem((CHIPS, 1, HALF), F32),
            vmem((CHIPS, 1, HALF), F32),
            vmem((2, 4, 4, 4, SHARE, HALF), BF16),
            vmem((2, 4, 2, REST, HALF), BF16),
            vmem((4, 4, 4, SHARE, ROWS), F32),
            vmem((4, 4, 4, SHARE, 128), F32),
            vmem((256, ROWS), F32),
            vmem((256, 128), F32),
            pltpu.SemaphoreType.DMA((5,)),
            pltpu.SemaphoreType.DMA((19,)),
            pltpu.SemaphoreType.DMA((69,)),
        ],
        compiler_params=pltpu.CompilerParams(
            collective_id=0, has_side_effects=True, vmem_limit_bytes=56 << 20),
    )(candidates, round_one, counts, chosen)
    return out[0] + out[2], out[1] + out[2]


def solution(mesh):
    in_specs = (P(("grp", "mem"), None), P(("grp", "mem"), None), P("grp", "mem"), P("grp", None))
    out_specs = (P(("grp", "mem")), P(("grp", "mem")))
    return jax.shard_map(body, mesh=mesh, in_specs=in_specs, out_specs=out_specs, check_vma=False)
```

```python
import jax
import jax.numpy as jnp
from jax import lax
from jax.experimental import pallas as pl
from jax.experimental.pallas import tpu as pltpu
from jax.sharding import PartitionSpec as P

MESH = pl.DeviceIdType.MESH
NT = (((1,), (1,)), ((), ()))
F32 = jnp.float32
BF16 = jnp.bfloat16
ALL = slice(None)

ROWS = 1024
WIDTH = 4096
HALF = WIDTH // 2
SLOTS = 64
PICKS = 128
CHIPS = 8
SHARE = PICKS // CHIPS
REST = 32
CUT = HALF * 3 // 4

RING = (0,)
EARLY = (0,)
SHARES = (
    (1, 0, 2, 0, 1024),
    (0, 2, 1, 1024, 1536),
    (2, 1, 0, 1536, 2048),
)


def place():
    g, m = lax.axis_index("grp"), lax.axis_index("mem")
    x = (g // 4) * 2 + (m // 2) % 2
    return x, m // 4, g % 4, m % 2


def device(x, y, z, c):
    return {"grp": (x // 2) * 4 + z, "mem": y * 4 + (x % 2) * 2 + c}


def fold(b):
    b = b.astype(F32)
    b = b * b
    total = b[:, 0:128]
    for k in range(128, b.shape[1], 128):
        total = total + b[:, k:k + 128]
    return total


def kernel(
    cand_ref, slot_ref, count_ref, chosen_ref, out_ref,
    CT, CH, A, S, CN, M, R, MO, RO, FIN, UN, D, NRM, DU, NU,
    local_sem, send_sem, recv_sem,
):
    x, y, z, c = place()
    pos3 = (x, y, z)
    xl = x % 2
    other = 1 - c
    me = lax.axis_index("mem")
    chip = y * 2 + xl
    sibling = device(x, y, z, other)
    used = {"send": 0, "recv": 0}

    def fresh(kind):
        used[kind] += 1
        return used[kind] - 1

    def send(src, dst, dev, out, into):
        pltpu.make_async_remote_copy(
            src_ref=src, dst_ref=dst, send_sem=send_sem.at[out], recv_sem=recv_sem.at[into],
            device_id=dev, device_id_type=MESH,
        ).start()

    def span(ref, out, into):
        return pltpu.make_async_remote_copy(
            src_ref=ref, dst_ref=ref, send_sem=send_sem.at[out], recv_sem=recv_sem.at[into],
            device_id=sibling, device_id_type=MESH,
        )

    def arrived(ref, into):
        span(ref, 0, into).wait_recv()

    leaving = []

    def leave(ref, out):
        leaving.append((ref, out))

    def device_at(dim, coord):
        p = list(pos3)
        p[dim] = coord
        return device(p[0], p[1], p[2], c)

    def in_group(dy, dx, dc):
        return device(x - xl + (xl + dx) % 2, (y + dy) % 4, z, (c + dc) % 2)

    partner, outer = x - xl + 1 - xl, (x + 4 - 1 + 2 * xl) % 4

    def neighbours(dim):
        if dim == 0:
            return ((partner, partner), (outer, outer))
        p = pos3[dim]
        return (((p + 1) % 4, (p + 3) % 4), ((p + 3) % 4, (p + 1) % 4))

    def far(dim):
        return (pos3[dim] + 2) % 4

    group_peers = [(dy, dx, dc) for dy in range(4) for dx in range(2) for dc in range(2) if dy or dx or dc]
    partners = [in_group(*o) for o in group_peers]
    partners += [device_at(2, (z + o) % 4) for o in (1, 2, 3)]
    partners += [device_at(0, outer), device_at(0, far(0))]
    barrier = pltpu.get_barrier_semaphore()
    for dev in partners:
        pl.semaphore_signal(barrier, inc=1, device_id=dev, device_id_type=MESH)
    small = [
        pltpu.make_async_copy(count_ref, CT, local_sem.at[3]),
        pltpu.make_async_copy(chosen_ref, CH, local_sem.at[4]),
    ]
    for cp in small:
        cp.start()
    mine = pltpu.make_async_copy(
        slot_ref.at[:, pl.ds(pl.multiple_of(c * HALF, HALF), HALF)], S.at[c], local_sem.at[0])
    mine.start()
    loads = []
    for h in range(2):
        cp = pltpu.make_async_copy(cand_ref.at[:, h * HALF:(h + 1) * HALF], A.at[h], local_sem.at[1 + h])
        cp.start()
        loads.append(cp)

    for cp in small:
        cp.wait()
    CN[me] = jnp.broadcast_to(CT[...], (8, 128))
    pl.semaphore_wait(barrier, len(partners))

    out_counts, in_counts = fresh("send"), fresh("recv")
    for o in group_peers:
        send(CN.at[me], CN.at[me], in_group(*o), out_counts, in_counts)
    leave(CN.at[0:15], out_counts)
    out_slots, in_slots = fresh("send"), fresh("recv")
    send(
        slot_ref.at[:, pl.ds(pl.multiple_of(other * HALF, HALF), HALF)], S.at[c], sibling,
        out_slots, in_slots)
    leave(S.at[0], out_slots)

    D[...] = jnp.zeros_like(D)
    NRM[...] = jnp.zeros_like(NRM)

    lane = lax.broadcasted_iota(jnp.int32, (1, 128), 1)
    row8 = lax.broadcasted_iota(jnp.int32, (8, 128), 0)
    row16 = lax.broadcasted_iota(jnp.int32, (16, 128), 0)
    row128 = lax.broadcasted_iota(jnp.int32, (128, 128), 0)
    chosen_col = jnp.transpose(jnp.broadcast_to(CH[...].astype(F32), (128, 128)))

    def below(p):
        return whole(jnp.sum(jnp.where(chosen_col < p, 1.0, 0.0), axis=0, keepdims=True))

    def whole(v):
        return v.astype(jnp.int32)

    def hot(rows, key):
        return jnp.where(rows == key, 1.0, 0.0).astype(BF16)

    arrived(CN.at[0:15], in_counts)
    cnt = jnp.max(CN[...].astype(F32), axis=1)
    off = jnp.zeros((16, 128), F32)
    for m in range(15):
        off = off + jnp.where(row16 > m, cnt[m:m + 1, :], 0.0)
    end = off + cnt

    def pick(table, index):
        return jnp.sum(jnp.where(row16 == index, table, 0.0), axis=0, keepdims=True)

    def amount(lo, hi, goal):
        return (hi - lo - (goal - lo + 1024) % 8 + 7) // 8

    first_off, last_end = pick(off, 2 * chip), pick(end, 2 * chip + 1)
    second = lane >= SLOTS
    within = lane % SLOTS
    spot = jnp.where(second, pick(off, 2 * chip + 1), first_off) + within.astype(F32)
    live = jnp.where(second, pick(cnt, 2 * chip + 1), pick(cnt, 2 * chip))
    alive = within.astype(F32) < live
    is_chosen = jnp.sum(jnp.where(chosen_col == spot, 1.0, 0.0), axis=0, keepdims=True) > 0.5
    q, q0, q1 = below(spot), below(first_off), below(last_end)
    u, u0 = whole(spot) - q, whole(first_off) - q0
    rank, nth = (u - u0) // 8, 15 - (u - u0) // 8
    apart = nth < amount(q0, q1, u % 8)
    key = jnp.where(is_chosen, (q % 8) * 16 + (q - q0) // 8, jnp.where(apart, -1, (u % 8) * 16 + nth))
    key_apart = jnp.where(is_chosen, -1, jnp.where(apart, u % 8, -1))
    hot_main = hot(row128, jnp.where(alive, key, -1))
    hot_apart = hot(row8, jnp.where(alive, key_apart, -1))

    mine.wait()
    arrived(S.at[0], in_slots)
    held = S[...].reshape(2 * SLOTS, HALF)
    M[...] = jnp.dot(hot_main, held, preferred_element_type=F32).astype(BF16).reshape(CHIPS, 16, HALF)
    out_swap, in_swap = fresh("send"), fresh("recv")
    chip_peers = [(dy, dx) for dy in range(4) for dx in range(2) if dy or dx]

    def target(dy, dx):
        return (y + dy) % 4 * 2 + (xl + dx) % 2

    for o in chip_peers:
        send(M.at[target(*o)], R.at[chip], in_group(*o, 0), out_swap, in_swap)
    leave(M.at[0:7], out_swap)
    MO[...] = jnp.dot(hot_apart, held, preferred_element_type=F32).reshape(CHIPS, 1, HALF)
    out_apart, in_apart = fresh("send"), fresh("recv")
    for o in chip_peers:
        send(MO.at[target(*o)], RO.at[chip], in_group(*o, 0), out_apart, in_apart)
    leave(MO.at[0:7], out_apart)
    R[chip] = M[chip]
    RO[chip] = MO[chip]

    def bounds(source):
        low = jnp.sum(jnp.where(row16 == 2 * source, off, 0.0), axis=0, keepdims=True)
        high = jnp.sum(jnp.where(row16 == 2 * source + 1, end, 0.0), axis=0, keepdims=True)
        ql, qh = below(low), below(high)
        return ql, qh, whole(low) - ql, whole(high) - qh

    ql, qh, ul, uh = bounds(lane // 16)
    nth = lane % 16
    at_q = ql + (chip - ql + 1024) % 8 + 8 * nth
    at_u = ul + (chip - ul + 1024) % 8 + 8 * (15 - nth)
    fits = nth >= amount(ql, qh, chip)
    row32 = lax.broadcasted_iota(jnp.int32, (REST, 128), 0)
    take_chosen = hot(row16, jnp.where(at_q < qh, at_q // 8, -1))
    take_rest = hot(row32, jnp.where(fits, jnp.where(at_u < uh, at_u // 8, -1), -1))
    ql, qh, ul, uh = bounds(lane)
    total = amount(ul, uh, chip)
    excess = amount(ql, qh, chip) + total > 16
    at_u = ul + (chip - ul + 1024) % 8 + 8 * (total - 1)
    take_apart = hot(row32, jnp.where(lane < CHIPS, jnp.where(excess, at_u // 8, -1), -1))

    for cp in loads:
        cp.wait()
    for i in range(8):
        rows = slice(i * 128, (i + 1) * 128)
        part = fold(A[0, rows, :]) + fold(A[1, rows, :])
        out_ref[2:3, rows] = jnp.sum(jnp.transpose(part), axis=0, keepdims=True)

    arrived(R.at[0:7], in_swap)
    got = R[...].reshape(CHIPS * 16, HALF)
    FIN[c, x, y, z] = jnp.dot(take_chosen, got, preferred_element_type=F32).astype(BF16)

    def block(share, s1, s2, s3, half=None):
        d1, d2, d3, lo, hi = share
        sel = [None] * 3
        sel[d1], sel[d2], sel[d3] = s1, s2, s3
        return FIN.at[(c if half is None else half, *sel, ALL, slice(lo, hi))]

    def blocks(share, *shape):
        lead = [slice(0, k) for k in shape]
        lead = [0] * (4 - len(lead)) + lead
        return FIN.at[(*lead, ALL, slice(share[3], share[4]))]

    n = len(SHARES)
    own = [tuple(pos3[s[k]] for k in range(3)) for s in SHARES]
    outs = [[fresh("send") for _ in range(3)] for _ in range(n)]
    planes_in = [[fresh("recv") for _ in range(4)] for _ in range(n)]
    for i, s in enumerate(SHARES):
        leave(blocks(s, 2, 3), outs[i][0])
        leave(blocks(s, 2, 4, 3), outs[i][1])
        leave(blocks(s, 2, 4, 4, 3), outs[i][2])
    out_own = fresh("send")

    def cast(i, k, index, coord, into):
        s = SHARES[i]
        ref = block(s, *index)
        send(ref, ref, device_at(s[k], coord), outs[i][k], into)

    def relay(i, k, index, plane):
        ref = block(SHARES[i], *index)
        send(ref, ref, sibling, outs[i][k], planes_in[i][plane])

    line_in = [[[fresh("recv") for _ in range(2)] for _ in range(4)] for _ in range(n)]
    first_in = [fresh("recv") for _ in range(n)]
    for i, s in enumerate(SHARES):
        for o in (1, 3, 2):
            cast(i, 0, own[i], (own[i][0] + o) % 4, first_in[i])
    for i in EARLY:
        for k, (goal, _) in enumerate(neighbours(SHARES[i][2])):
            cast(i, 2, own[i], goal, line_in[i][0][k])
    for i, s in enumerate(SHARES):
        ref = block(s, *own[i])
        send(ref, ref, sibling, out_own, planes_in[i][0])
    leave(FIN.at[0, 0, 0, 0], out_own)

    rest = jnp.dot(take_rest, got, preferred_element_type=F32)
    arrived(RO.at[0:7], in_apart)
    lone = RO[...].reshape(CHIPS, HALF).astype(BF16)
    lone = jnp.concatenate([lone, jnp.zeros((128 - CHIPS, HALF), BF16)], axis=0)
    rest = rest + jnp.dot(take_apart, lone, preferred_element_type=F32)
    UN[c, y, xl] = rest.astype(BF16)
    left, right = slice(0, CUT), slice(CUT, HALF)
    un_in = fresh("recv")
    un_out = fresh("send")
    leave(UN.at[0], un_out)
    outs_y, ins_y = fresh("send"), fresh("recv")
    outs_x, ins_x = fresh("send"), fresh("recv")
    outs_yx, ins_yx = fresh("send"), fresh("recv")
    outs_xy, ins_xy = fresh("send"), fresh("recv")

    def pass_on(sel, dev, out, into):
        ref = UN.at[sel]
        send(ref, ref, dev, out, into)

    for o in (1, 3, 2):
        pass_on((c, y, xl, ALL, left), in_group(o, 0, 0), outs_y, ins_y)
    leave(UN.at[0, 0:3, 0, :, left], outs_y)
    pass_on((c, y, xl, ALL, right), in_group(0, 1, 0), outs_x, ins_x)
    leave(UN.at[0, 0, 0, :, right], outs_x)
    pass_on((c, y, xl), sibling, un_out, un_in)

    lines = [[None] * 4 for _ in range(n)]
    second_in = [[fresh("recv") for _ in range(3)] for _ in range(n)]

    def third(i, j, coord):
        s = SHARES[i]
        lines[i][j] = coord
        for k, (goal, _) in enumerate(neighbours(s[2])):
            cast(i, 2, (ALL, coord, own[i][2]), goal, line_in[i][j][k])

    for i in (1, 2, 0):
        s = SHARES[i]
        arrived(blocks(s, 3), first_in[i])
        row = (ALL, own[i][1], own[i][2])
        for k, (goal, _) in enumerate(neighbours(s[1])):
            cast(i, 1, row, goal, second_in[i][k])
        if s[1] not in RING:
            cast(i, 1, row, far(s[1]), second_in[i][2])
    for i, s in enumerate(SHARES):
        if i in EARLY:
            lines[i][0] = own[i][1]
            for o in (1, 3, 2):
                for k, (goal, _) in enumerate(neighbours(s[2])):
                    cast(i, 2, ((own[i][0] + o) % 4, own[i][1], own[i][2]), goal, line_in[i][0][k])
        else:
            third(i, 0, own[i][1])
    for i, s in enumerate(SHARES):
        for o in (1, 3, 2):
            relay(i, 0, ((own[i][0] + o) % 4, own[i][1], own[i][2]), 0)

    def more(j):
        for i, s in enumerate(SHARES):
            arrived(blocks(s, 4), second_in[i][j])
            coord = neighbours(s[1])[j][1] if j < 2 else far(s[1])
            row = (ALL, coord, own[i][2])
            if s[1] == 0 and j == 0:
                cast(i, 1, row, outer, second_in[i][2])
            elif s[1] in RING and s[1] != 0 and j < 2:
                half = (slice(2 * j, 2 * j + 2), coord, own[i][2])
                cast(i, 1, half, neighbours(s[1])[j][0], second_in[i][2])
            third(i, 1 + j, coord)
            relay(i, 1, row, 0)

    def spread(i, d1, d2, d3):
        sel = [None] * 3
        sel[SHARES[i][0]], sel[SHARES[i][1]], sel[SHARES[i][2]] = d1, d2, d3
        return tuple(sel) + (ALL,)

    def multiply(i, h, parts):
        lo, hi = SHARES[i][3:]
        count = 256 // len(parts)
        rows = [FIN[(h,) + sel + (slice(lo, hi),)].reshape(count, hi - lo) for sel in parts]
        b = rows[0] if len(rows) == 1 else jnp.concatenate(rows, axis=0)
        dots = lax.dot_general(b, A[h, :, lo:hi], NT, preferred_element_type=F32)
        norms = fold(b)
        for p, sel in enumerate(parts):
            at = slice(p * count, (p + 1) * count)
            where = sel + (ALL,)
            D[where] += dots[at].reshape(D[where].shape)
            NRM[where] += norms[at].reshape(NRM[where].shape)

    far_in = [[fresh("recv") for _ in range(4)] for _ in range(n)]

    def line(j):
        for i, s in enumerate(SHARES):
            for k, (goal, origin) in enumerate(neighbours(s[2])):
                arrived(blocks(s, 4), line_in[i][j][k])
                row = (ALL, lines[i][j], origin)
                if s[2] == 0:
                    if k == 0:
                        cast(i, 2, row, outer, far_in[i][j])
                elif (j < 2) == (k == 0):
                    cast(i, 2, row, goal, far_in[i][j])
                relay(i, 2, row, 1 + j // 2)

    def parts(i, k):
        s = SHARES[i]
        if k in (0, 3):
            return [spread(i, ALL, ALL, far(s[2]) if k else own[i][2])]
        js = (0, 1) if k == 1 else (2, 3)
        return [spread(i, ALL, lines[i][j], origin) for j in js for _, origin in neighbours(s[2])]

    def own_half(k):
        for i in (1, 2, 0):
            multiply(i, c, parts(i, k))

    def other_half(k):
        for i in (1, 2, 0):
            arrived(blocks(SHARES[i], 4, 4), planes_in[i][k])
            multiply(i, other, parts(i, k))

    def far_line(j):
        for i in (1, 2, 0):
            s = SHARES[i]
            arrived(blocks(s, 4), far_in[i][j])
            relay(i, 2, (ALL, lines[i][j], far(s[2])), 3)

    def un_dots(h):
        b = UN[h].reshape(256, HALF)
        return lax.dot_general(b, A[h], NT, preferred_element_type=F32), fold(b)

    def un_own():
        DU[...], NU[...] = un_dots(c)

    def un_other():
        arrived(UN.at[0], un_in)
        dots, norms = un_dots(other)
        norms = jnp.sum(NU[...] + norms, axis=1, keepdims=True)
        out_ref[0:1, :] = jnp.min(norms - 2.0 * (DU[...] + dots), axis=0, keepdims=True)

    def un_collect():
        arrived(UN.at[0, :, 0, :, left], ins_yx)
        pass_on((c, ALL, 1 - xl, ALL, left), sibling, un_out, un_in)
        arrived(UN.at[0, 0:3, :, :, right], ins_xy)
        for o in (1, 2, 3):
            pass_on((c, (y + o) % 4, ALL, ALL, right), sibling, un_out, un_in)

    more(0)
    more(1)
    arrived(UN.at[0, 0, 0, :, right], ins_x)
    for o in (1, 3, 2):
        pass_on((c, y, ALL, ALL, right), in_group(o, 0, 0), outs_xy, ins_xy)
    leave(UN.at[0, 0:3, :, :, right], outs_xy)
    pass_on((c, y, 1 - xl, ALL, right), sibling, un_out, un_in)
    arrived(UN.at[0, 0:3, 0, :, left], ins_y)
    pass_on((c, ALL, xl, ALL, left), in_group(0, 1, 0), outs_yx, ins_yx)
    leave(UN.at[0, :, 0, :, left], outs_yx)
    for o in (1, 2, 3):
        pass_on((c, (y + o) % 4, xl, ALL, left), sibling, un_out, un_in)
    line(0)
    more(2)
    own_half(0)
    line(1)
    other_half(0)
    line(2)
    own_half(1)
    far_line(0)
    other_half(1)
    line(3)
    un_collect()
    un_own()
    far_line(1)
    own_half(2)
    far_line(2)
    other_half(2)
    far_line(3)
    un_other()
    own_half(3)
    other_half(3)

    def smallest(dots, norms):
        total = jnp.sum(norms.reshape(-1, 128), axis=1, keepdims=True)
        return jnp.min(total - 2.0 * dots.reshape(-1, ROWS), axis=0, keepdims=True)

    best = jnp.full((1, ROWS), jnp.inf, F32)
    for i in range(4):
        best = jnp.minimum(best, smallest(D[i], NRM[i]))
    near = out_ref[0:1, :]
    for i in range(2):
        px = x - xl + i
        near = jnp.minimum(near, smallest(D[px, :, z], NRM[px, :, z]))
    out_ref[0:1, :] = near
    out_ref[1:2, :] = best
    for ref, out in leaving:
        span(ref, out, 0).wait_send()


def body(candidates, round_one, counts, chosen):
    vmem = pltpu.VMEM
    out = pl.pallas_call(
        kernel,
        out_shape=jax.ShapeDtypeStruct((3, ROWS), F32),
        in_specs=[
            pl.BlockSpec(memory_space=pl.ANY),
            pl.BlockSpec(memory_space=pl.ANY),
            pl.BlockSpec(memory_space=pl.ANY),
            pl.BlockSpec(memory_space=pl.ANY),
        ],
        out_specs=pl.BlockSpec(memory_space=vmem),
        scratch_shapes=[
            vmem((1, 1), jnp.int32),
            vmem((1, PICKS), jnp.int32),
            vmem((2, ROWS, HALF), BF16),
            vmem((2, SLOTS, HALF), BF16),
            vmem((16, 8, 128), jnp.int32),
            vmem((CHIPS, 16, HALF), BF16),
            vmem((CHIPS, 16, HALF), BF16),
            vmem((CHIPS, 1, HALF), F32),
            vmem((CHIPS, 1, HALF), F32),
            vmem((2, 4, 4, 4, SHARE, HALF), BF16),
            vmem((2, 4, 2, REST, HALF), BF16),
            vmem((4, 4, 4, SHARE, ROWS), F32),
            vmem((4, 4, 4, SHARE, 128), F32),
            vmem((256, ROWS), F32),
            vmem((256, 128), F32),
            pltpu.SemaphoreType.DMA((5,)),
            pltpu.SemaphoreType.DMA((19,)),
            pltpu.SemaphoreType.DMA((69,)),
        ],
        compiler_params=pltpu.CompilerParams(
            collective_id=0, has_side_effects=True, vmem_limit_bytes=56 << 20),
    )(candidates, round_one, counts, chosen)
    return out[0] + out[2], out[1] + out[2]


def solution(mesh):
    in_specs = (P(("grp", "mem"), None), P(("grp", "mem"), None), P("grp", "mem"), P("grp", None))
    out_specs = (P(("grp", "mem")), P(("grp", "mem")))
    return jax.shard_map(body, mesh=mesh, in_specs=in_specs, out_specs=out_specs, check_vma=False)
```

```python
import jax
import jax.numpy as jnp
from jax import lax
from jax.experimental import pallas as pl
from jax.experimental.pallas import tpu as pltpu
from jax.sharding import PartitionSpec as P

MESH = pl.DeviceIdType.MESH
NT = (((1,), (1,)), ((), ()))
F32 = jnp.float32
BF16 = jnp.bfloat16
ALL = slice(None)

ROWS = 1024
WIDTH = 4096
HALF = WIDTH // 2
SLOTS = 64
PICKS = 128
CHIPS = 8
SHARE = PICKS // CHIPS
REST = 32
CUT = HALF * 3 // 4

RING = (0,)
EARLY = (0,)
SHARES = (
    (1, 0, 2, 0, 1024),
    (0, 2, 1, 1024, 1536),
    (2, 1, 0, 1536, 2048),
)


def place():
    g, m = lax.axis_index("grp"), lax.axis_index("mem")
    x = (g // 4) * 2 + (m // 2) % 2
    return x, m // 4, g % 4, m % 2


def device(x, y, z, c):
    return {"grp": (x // 2) * 4 + z, "mem": y * 4 + (x % 2) * 2 + c}


def fold(b):
    b = b.astype(F32)
    b = b * b
    total = b[:, 0:128]
    for k in range(128, b.shape[1], 128):
        total = total + b[:, k:k + 128]
    return total


def kernel(
    cand_ref, slot_ref, count_ref, chosen_ref, out_ref,
    CT, CH, A, S, CN, M, R, MO, RO, FIN, UN, D, NRM, DU, NU,
    local_sem, send_sem, recv_sem,
):
    x, y, z, c = place()
    pos3 = (x, y, z)
    xl = x % 2
    other = 1 - c
    me = lax.axis_index("mem")
    chip = y * 2 + xl
    sibling = device(x, y, z, other)
    used = {"send": 0, "recv": 0}

    def fresh(kind):
        used[kind] += 1
        return used[kind] - 1

    def send(src, dst, dev, out, into):
        pltpu.make_async_remote_copy(
            src_ref=src, dst_ref=dst, send_sem=send_sem.at[out], recv_sem=recv_sem.at[into],
            device_id=dev, device_id_type=MESH,
        ).start()

    def span(ref, out, into):
        return pltpu.make_async_remote_copy(
            src_ref=ref, dst_ref=ref, send_sem=send_sem.at[out], recv_sem=recv_sem.at[into],
            device_id=sibling, device_id_type=MESH,
        )

    def arrived(ref, into):
        span(ref, 0, into).wait_recv()

    leaving = []

    def leave(ref, out):
        leaving.append((ref, out))

    def device_at(dim, coord):
        p = list(pos3)
        p[dim] = coord
        return device(p[0], p[1], p[2], c)

    def in_group(dy, dx, dc):
        return device(x - xl + (xl + dx) % 2, (y + dy) % 4, z, (c + dc) % 2)

    partner, outer = x - xl + 1 - xl, (x + 4 - 1 + 2 * xl) % 4

    def neighbours(dim):
        if dim == 0:
            return ((partner, partner), (outer, outer))
        p = pos3[dim]
        return (((p + 1) % 4, (p + 3) % 4), ((p + 3) % 4, (p + 1) % 4))

    def far(dim):
        return (pos3[dim] + 2) % 4

    group_peers = [(dy, dx, dc) for dy in range(4) for dx in range(2) for dc in range(2) if dy or dx or dc]
    partners = [in_group(*o) for o in group_peers]
    partners += [device_at(2, (z + o) % 4) for o in (1, 2, 3)]
    partners += [device_at(0, outer), device_at(0, far(0))]
    barrier = pltpu.get_barrier_semaphore()
    for dev in partners:
        pl.semaphore_signal(barrier, inc=1, device_id=dev, device_id_type=MESH)
    small = [
        pltpu.make_async_copy(count_ref, CT, local_sem.at[3]),
        pltpu.make_async_copy(chosen_ref, CH, local_sem.at[4]),
    ]
    for cp in small:
        cp.start()
    mine = pltpu.make_async_copy(
        slot_ref.at[:, pl.ds(pl.multiple_of(c * HALF, HALF), HALF)], S.at[c], local_sem.at[0])
    mine.start()
    loads = []
    for h in range(2):
        cp = pltpu.make_async_copy(cand_ref.at[:, h * HALF:(h + 1) * HALF], A.at[h], local_sem.at[1 + h])
        cp.start()
        loads.append(cp)

    for cp in small:
        cp.wait()
    CN[me] = jnp.broadcast_to(CT[...], (8, 128))
    pl.semaphore_wait(barrier, len(partners))

    out_counts, in_counts = fresh("send"), fresh("recv")
    for o in group_peers:
        send(CN.at[me], CN.at[me], in_group(*o), out_counts, in_counts)
    leave(CN.at[0:15], out_counts)
    out_slots, in_slots = fresh("send"), fresh("recv")
    send(
        slot_ref.at[:, pl.ds(pl.multiple_of(other * HALF, HALF), HALF)], S.at[c], sibling,
        out_slots, in_slots)
    leave(S.at[0], out_slots)

    D[...] = jnp.zeros_like(D)
    NRM[...] = jnp.zeros_like(NRM)

    lane = lax.broadcasted_iota(jnp.int32, (1, 128), 1)
    row8 = lax.broadcasted_iota(jnp.int32, (8, 128), 0)
    row16 = lax.broadcasted_iota(jnp.int32, (16, 128), 0)
    row128 = lax.broadcasted_iota(jnp.int32, (128, 128), 0)
    chosen_col = jnp.transpose(jnp.broadcast_to(CH[...].astype(F32), (128, 128)))

    def below(p):
        return whole(jnp.sum(jnp.where(chosen_col < p, 1.0, 0.0), axis=0, keepdims=True))

    def whole(v):
        return v.astype(jnp.int32)

    def hot(rows, key):
        return jnp.where(rows == key, 1.0, 0.0).astype(BF16)

    arrived(CN.at[0:15], in_counts)
    cnt = jnp.max(CN[...].astype(F32), axis=1)
    off = jnp.zeros((16, 128), F32)
    for m in range(15):
        off = off + jnp.where(row16 > m, cnt[m:m + 1, :], 0.0)
    end = off + cnt

    def pick(table, index):
        return jnp.sum(jnp.where(row16 == index, table, 0.0), axis=0, keepdims=True)

    def amount(lo, hi, goal):
        return (hi - lo - (goal - lo + 1024) % 8 + 7) // 8

    first_off, last_end = pick(off, 2 * chip), pick(end, 2 * chip + 1)
    second = lane >= SLOTS
    within = lane % SLOTS
    spot = jnp.where(second, pick(off, 2 * chip + 1), first_off) + within.astype(F32)
    live = jnp.where(second, pick(cnt, 2 * chip + 1), pick(cnt, 2 * chip))
    alive = within.astype(F32) < live
    is_chosen = jnp.sum(jnp.where(chosen_col == spot, 1.0, 0.0), axis=0, keepdims=True) > 0.5
    q, q0, q1 = below(spot), below(first_off), below(last_end)
    u, u0 = whole(spot) - q, whole(first_off) - q0
    rank, nth = (u - u0) // 8, 15 - (u - u0) // 8
    apart = nth < amount(q0, q1, u % 8)
    key = jnp.where(is_chosen, (q % 8) * 16 + (q - q0) // 8, jnp.where(apart, -1, (u % 8) * 16 + nth))
    key_apart = jnp.where(is_chosen, -1, jnp.where(apart, u % 8, -1))
    hot_main = hot(row128, jnp.where(alive, key, -1))
    hot_apart = hot(row8, jnp.where(alive, key_apart, -1))

    mine.wait()
    arrived(S.at[0], in_slots)
    held = S[...].reshape(2 * SLOTS, HALF)
    M[...] = jnp.dot(hot_main, held, preferred_element_type=F32).astype(BF16).reshape(CHIPS, 16, HALF)
    out_swap, in_swap = fresh("send"), fresh("recv")
    chip_peers = [(dy, dx) for dy in range(4) for dx in range(2) if dy or dx]

    def target(dy, dx):
        return (y + dy) % 4 * 2 + (xl + dx) % 2

    for o in chip_peers:
        send(M.at[target(*o)], R.at[chip], in_group(*o, 0), out_swap, in_swap)
    leave(M.at[0:7], out_swap)
    MO[...] = jnp.dot(hot_apart, held, preferred_element_type=F32).reshape(CHIPS, 1, HALF)
    out_apart, in_apart = fresh("send"), fresh("recv")
    for o in chip_peers:
        send(MO.at[target(*o)], RO.at[chip], in_group(*o, 0), out_apart, in_apart)
    leave(MO.at[0:7], out_apart)
    R[chip] = M[chip]
    RO[chip] = MO[chip]

    def bounds(source):
        low = jnp.sum(jnp.where(row16 == 2 * source, off, 0.0), axis=0, keepdims=True)
        high = jnp.sum(jnp.where(row16 == 2 * source + 1, end, 0.0), axis=0, keepdims=True)
        ql, qh = below(low), below(high)
        return ql, qh, whole(low) - ql, whole(high) - qh

    ql, qh, ul, uh = bounds(lane // 16)
    nth = lane % 16
    at_q = ql + (chip - ql + 1024) % 8 + 8 * nth
    at_u = ul + (chip - ul + 1024) % 8 + 8 * (15 - nth)
    fits = nth >= amount(ql, qh, chip)
    row32 = lax.broadcasted_iota(jnp.int32, (REST, 128), 0)
    take_chosen = hot(row16, jnp.where(at_q < qh, at_q // 8, -1))
    take_rest = hot(row32, jnp.where(fits, jnp.where(at_u < uh, at_u // 8, -1), -1))
    ql, qh, ul, uh = bounds(lane)
    total = amount(ul, uh, chip)
    excess = amount(ql, qh, chip) + total > 16
    at_u = ul + (chip - ul + 1024) % 8 + 8 * (total - 1)
    take_apart = hot(row32, jnp.where(lane < CHIPS, jnp.where(excess, at_u // 8, -1), -1))

    for cp in loads:
        cp.wait()
    for i in range(8):
        rows = slice(i * 128, (i + 1) * 128)
        part = fold(A[0, rows, :]) + fold(A[1, rows, :])
        out_ref[2:3, rows] = jnp.sum(jnp.transpose(part), axis=0, keepdims=True)

    arrived(R.at[0:7], in_swap)
    got = R[...].reshape(CHIPS * 16, HALF)
    FIN[c, x, y, z] = jnp.dot(take_chosen, got, preferred_element_type=F32).astype(BF16)

    def block(share, s1, s2, s3, half=None):
        d1, d2, d3, lo, hi = share
        sel = [None] * 3
        sel[d1], sel[d2], sel[d3] = s1, s2, s3
        return FIN.at[(c if half is None else half, *sel, ALL, slice(lo, hi))]

    def blocks(share, *shape):
        lead = [slice(0, k) for k in shape]
        lead = [0] * (4 - len(lead)) + lead
        return FIN.at[(*lead, ALL, slice(share[3], share[4]))]

    n = len(SHARES)
    own = [tuple(pos3[s[k]] for k in range(3)) for s in SHARES]
    outs = [[fresh("send") for _ in range(3)] for _ in range(n)]
    planes_in = [[fresh("recv") for _ in range(4)] for _ in range(n)]
    for i, s in enumerate(SHARES):
        leave(blocks(s, 2, 3), outs[i][0])
        leave(blocks(s, 2, 4, 3), outs[i][1])
        leave(blocks(s, 2, 4, 4, 3), outs[i][2])
    out_own = fresh("send")

    def cast(i, k, index, coord, into):
        s = SHARES[i]
        ref = block(s, *index)
        send(ref, ref, device_at(s[k], coord), outs[i][k], into)

    def relay(i, k, index, plane):
        ref = block(SHARES[i], *index)
        send(ref, ref, sibling, outs[i][k], planes_in[i][plane])

    line_in = [[fresh("recv") for _ in range(4)] for _ in range(n)]
    first_in = [fresh("recv") for _ in range(n)]
    for i, s in enumerate(SHARES):
        for o in (1, 3, 2):
            cast(i, 0, own[i], (own[i][0] + o) % 4, first_in[i])
    for i in EARLY:
        for k, (goal, _) in enumerate(neighbours(SHARES[i][2])):
            cast(i, 2, own[i], goal, line_in[i][0])
    for i, s in enumerate(SHARES):
        ref = block(s, *own[i])
        send(ref, ref, sibling, out_own, planes_in[i][0])
    leave(FIN.at[0, 0, 0, 0], out_own)

    rest = jnp.dot(take_rest, got, preferred_element_type=F32)
    arrived(RO.at[0:7], in_apart)
    lone = RO[...].reshape(CHIPS, HALF).astype(BF16)
    lone = jnp.concatenate([lone, jnp.zeros((128 - CHIPS, HALF), BF16)], axis=0)
    rest = rest + jnp.dot(take_apart, lone, preferred_element_type=F32)
    UN[c, y, xl] = rest.astype(BF16)
    left, right = slice(0, CUT), slice(CUT, HALF)
    un_in = fresh("recv")
    un_out = fresh("send")
    leave(UN.at[0], un_out)
    outs_y, ins_y = fresh("send"), fresh("recv")
    outs_x, ins_x = fresh("send"), fresh("recv")
    outs_yx, ins_yx = fresh("send"), fresh("recv")
    outs_xy, ins_xy = fresh("send"), fresh("recv")

    def pass_on(sel, dev, out, into):
        ref = UN.at[sel]
        send(ref, ref, dev, out, into)

    for o in (1, 3, 2):
        pass_on((c, y, xl, ALL, left), in_group(o, 0, 0), outs_y, ins_y)
    leave(UN.at[0, 0:3, 0, :, left], outs_y)
    pass_on((c, y, xl, ALL, right), in_group(0, 1, 0), outs_x, ins_x)
    leave(UN.at[0, 0, 0, :, right], outs_x)
    pass_on((c, y, xl), sibling, un_out, un_in)

    lines = [[None] * 4 for _ in range(n)]
    second_in = [[fresh("recv") for _ in range(3)] for _ in range(n)]

    def third(i, j, coord):
        s = SHARES[i]
        lines[i][j] = coord
        for k, (goal, _) in enumerate(neighbours(s[2])):
            cast(i, 2, (ALL, coord, own[i][2]), goal, line_in[i][j])

    for i in (1, 2, 0):
        s = SHARES[i]
        arrived(blocks(s, 3), first_in[i])
        row = (ALL, own[i][1], own[i][2])
        for k, (goal, _) in enumerate(neighbours(s[1])):
            cast(i, 1, row, goal, second_in[i][k])
        if s[1] not in RING:
            cast(i, 1, row, far(s[1]), second_in[i][2])
    for i, s in enumerate(SHARES):
        if i in EARLY:
            lines[i][0] = own[i][1]
            for o in (1, 3, 2):
                for k, (goal, _) in enumerate(neighbours(s[2])):
                    cast(i, 2, ((own[i][0] + o) % 4, own[i][1], own[i][2]), goal, line_in[i][0])
        else:
            third(i, 0, own[i][1])
    for i, s in enumerate(SHARES):
        for o in (1, 3, 2):
            relay(i, 0, ((own[i][0] + o) % 4, own[i][1], own[i][2]), 0)

    def more(j):
        for i, s in enumerate(SHARES):
            arrived(blocks(s, 4), second_in[i][j])
            coord = neighbours(s[1])[j][1] if j < 2 else far(s[1])
            row = (ALL, coord, own[i][2])
            if s[1] == 0 and j == 0:
                cast(i, 1, row, outer, second_in[i][2])
            elif s[1] in RING and s[1] != 0 and j < 2:
                half = (slice(2 * j, 2 * j + 2), coord, own[i][2])
                cast(i, 1, half, neighbours(s[1])[j][0], second_in[i][2])
            third(i, 1 + j, coord)
            relay(i, 1, row, 0)

    def spread(i, d1, d2, d3):
        sel = [None] * 3
        sel[SHARES[i][0]], sel[SHARES[i][1]], sel[SHARES[i][2]] = d1, d2, d3
        return tuple(sel) + (ALL,)

    def multiply(i, h, parts):
        lo, hi = SHARES[i][3:]
        count = 256 // len(parts)
        rows = [FIN[(h,) + sel + (slice(lo, hi),)].reshape(count, hi - lo) for sel in parts]
        b = rows[0] if len(rows) == 1 else jnp.concatenate(rows, axis=0)
        dots = lax.dot_general(b, A[h, :, lo:hi], NT, preferred_element_type=F32)
        norms = fold(b)
        for p, sel in enumerate(parts):
            at = slice(p * count, (p + 1) * count)
            where = sel + (ALL,)
            D[where] += dots[at].reshape(D[where].shape)
            NRM[where] += norms[at].reshape(NRM[where].shape)

    far_in = [[fresh("recv") for _ in range(4)] for _ in range(n)]

    def line(j):
        for i, s in enumerate(SHARES):
            arrived(blocks(s, 2, 4), line_in[i][j])
            for k, (goal, origin) in enumerate(neighbours(s[2])):
                row = (ALL, lines[i][j], origin)
                if s[2] == 0:
                    if k == 0:
                        cast(i, 2, row, outer, far_in[i][j])
                elif (j < 2) == (k == 0):
                    cast(i, 2, row, goal, far_in[i][j])
                relay(i, 2, row, 1 + j // 2)

    def parts(i, k):
        s = SHARES[i]
        if k in (0, 3):
            return [spread(i, ALL, ALL, far(s[2]) if k else own[i][2])]
        js = (0, 1) if k == 1 else (2, 3)
        return [spread(i, ALL, lines[i][j], origin) for j in js for _, origin in neighbours(s[2])]

    def own_half(k):
        for i in (1, 2, 0):
            multiply(i, c, parts(i, k))

    def other_half(k):
        for i in (1, 2, 0):
            arrived(blocks(SHARES[i], 4, 4), planes_in[i][k])
            multiply(i, other, parts(i, k))

    def far_line(j):
        for i in (1, 2, 0):
            s = SHARES[i]
            arrived(blocks(s, 4), far_in[i][j])
            relay(i, 2, (ALL, lines[i][j], far(s[2])), 3)

    def un_dots(h):
        b = UN[h].reshape(256, HALF)
        return lax.dot_general(b, A[h], NT, preferred_element_type=F32), fold(b)

    def un_own():
        DU[...], NU[...] = un_dots(c)

    def un_other():
        arrived(UN.at[0], un_in)
        dots, norms = un_dots(other)
        norms = jnp.sum(NU[...] + norms, axis=1, keepdims=True)
        out_ref[0:1, :] = jnp.min(norms - 2.0 * (DU[...] + dots), axis=0, keepdims=True)

    def un_collect():
        arrived(UN.at[0, :, 0, :, left], ins_yx)
        pass_on((c, ALL, 1 - xl, ALL, left), sibling, un_out, un_in)
        arrived(UN.at[0, 0:3, :, :, right], ins_xy)
        for o in (1, 2, 3):
            pass_on((c, (y + o) % 4, ALL, ALL, right), sibling, un_out, un_in)

    more(0)
    more(1)
    arrived(UN.at[0, 0, 0, :, right], ins_x)
    for o in (1, 3, 2):
        pass_on((c, y, ALL, ALL, right), in_group(o, 0, 0), outs_xy, ins_xy)
    leave(UN.at[0, 0:3, :, :, right], outs_xy)
    pass_on((c, y, 1 - xl, ALL, right), sibling, un_out, un_in)
    arrived(UN.at[0, 0:3, 0, :, left], ins_y)
    pass_on((c, ALL, xl, ALL, left), in_group(0, 1, 0), outs_yx, ins_yx)
    leave(UN.at[0, :, 0, :, left], outs_yx)
    for o in (1, 2, 3):
        pass_on((c, (y + o) % 4, xl, ALL, left), sibling, un_out, un_in)
    line(0)
    more(2)
    own_half(0)
    line(1)
    other_half(0)
    line(2)
    own_half(1)
    far_line(0)
    other_half(1)
    line(3)
    un_collect()
    un_own()
    far_line(1)
    own_half(2)
    far_line(2)
    other_half(2)
    far_line(3)
    un_other()
    own_half(3)
    other_half(3)

    def smallest(dots, norms):
        total = jnp.sum(norms.reshape(-1, 128), axis=1, keepdims=True)
        return jnp.min(total - 2.0 * dots.reshape(-1, ROWS), axis=0, keepdims=True)

    best = jnp.full((1, ROWS), jnp.inf, F32)
    for i in range(4):
        best = jnp.minimum(best, smallest(D[i], NRM[i]))
    near = out_ref[0:1, :]
    for i in range(2):
        px = x - xl + i
        near = jnp.minimum(near, smallest(D[px, :, z], NRM[px, :, z]))
    out_ref[0:1, :] = near
    out_ref[1:2, :] = best
    for ref, out in leaving:
        span(ref, out, 0).wait_send()


def body(candidates, round_one, counts, chosen):
    vmem = pltpu.VMEM
    out = pl.pallas_call(
        kernel,
        out_shape=jax.ShapeDtypeStruct((3, ROWS), F32),
        in_specs=[
            pl.BlockSpec(memory_space=pl.ANY),
            pl.BlockSpec(memory_space=pl.ANY),
            pl.BlockSpec(memory_space=pl.ANY),
            pl.BlockSpec(memory_space=pl.ANY),
        ],
        out_specs=pl.BlockSpec(memory_space=vmem),
        scratch_shapes=[
            vmem((1, 1), jnp.int32),
            vmem((1, PICKS), jnp.int32),
            vmem((2, ROWS, HALF), BF16),
            vmem((2, SLOTS, HALF), BF16),
            vmem((16, 8, 128), jnp.int32),
            vmem((CHIPS, 16, HALF), BF16),
            vmem((CHIPS, 16, HALF), BF16),
            vmem((CHIPS, 1, HALF), F32),
            vmem((CHIPS, 1, HALF), F32),
            vmem((2, 4, 4, 4, SHARE, HALF), BF16),
            vmem((2, 4, 2, REST, HALF), BF16),
            vmem((4, 4, 4, SHARE, ROWS), F32),
            vmem((4, 4, 4, SHARE, 128), F32),
            vmem((256, ROWS), F32),
            vmem((256, 128), F32),
            pltpu.SemaphoreType.DMA((5,)),
            pltpu.SemaphoreType.DMA((19,)),
            pltpu.SemaphoreType.DMA((57,)),
        ],
        compiler_params=pltpu.CompilerParams(
            collective_id=0, has_side_effects=True, vmem_limit_bytes=56 << 20),
    )(candidates, round_one, counts, chosen)
    return out[0] + out[2], out[1] + out[2]


def solution(mesh):
    in_specs = (P(("grp", "mem"), None), P(("grp", "mem"), None), P("grp", "mem"), P("grp", None))
    out_specs = (P(("grp", "mem")), P(("grp", "mem")))
    return jax.shard_map(body, mesh=mesh, in_specs=in_specs, out_specs=out_specs, check_vma=False)
```
